256 devices in a mesh: dp: 8 (over y, core), cent: 32 (over z, x).
Axes of the slice: x: 4, y: 4, z: 8, core: 2. Of those that a mesh axis runs over, the one named last changes fastest.
Arguments:
- features: bfloat16 [8192, 1024], P('dp', 'cent'), may hold values from -128 to 128
- centroids: bfloat16 [65536, 1024], P('cent'), may hold values from -2 to 2
- row_weight: float32 [8192], P('dp'), may hold values from 0.5 to 18
- centroid_share: float32 [65536], P('cent'), may hold values from 0.5 to 18
Outputs:
- centroid_means: float32 [1024, 65536], P('dp', 'cent')
- centroid_mass: float32 [65536], P('cent')
The draws below stay inside these ranges and needn't reach their ends.
All inputs are finite; a program needn't handle non-finite values.
Results may differ from the reference program's by a relative error of at most 0.001.
The reference program's roundings to bfloat16 on the way (of `weights`) count: a program that leaves them out, or rounds other values in their place, can miss the bound.
Values may be sent and summed in bfloat16 or wider, within the bound.
No kernel may reach another device: no remote copies, remote signals or barrier semaphores. Data moves between devices by JAX's collectives and lax.ppermute only.
A program may use at most 64 MiB of HBM per device.

```python
import math
import jax
import jax.numpy as jnp
from jax import lax

D = 1024
K_DEV = 2048
ITERS = 3
ROWS = 8192
CENTROIDS = 65536
N_CENT = 32


def shared_draw(key):
    key_cent = jax.random.fold_in(key, 101)
    key_feat = jax.random.fold_in(key, 202)
    spread = 2.0 / math.sqrt(D)
    centers = jnp.clip(jax.random.normal(key_cent, (CENTROIDS, D), jnp.float32), -6.0, 6.0) * spread
    centers = centers.astype(jnp.bfloat16).astype(jnp.float32)
    base = jnp.clip(jax.random.normal(jax.random.fold_in(key_feat, 1), (ROWS, D), jnp.float32), -6.0, 6.0)
    feats = base
    return (feats, centers)


def rising_draw(key, length):
    position = jnp.arange(length).astype(jnp.float32) / length
    factor = jnp.exp(jax.random.uniform(key, (length,), jnp.float32, math.log(0.5), math.log(2.0)))
    return factor * jnp.exp(position * math.log(3.0))


def draw_features(key, part):
    return shared_draw(key)[0].astype(jnp.bfloat16)


def draw_centroids(key, part):
    return shared_draw(key)[1].astype(jnp.bfloat16)


def draw_row_weight(key, part):
    return rising_draw(jax.random.fold_in(key, 303), ROWS)


def draw_centroid_share(key, part):
    return rising_draw(jax.random.fold_in(key, 404), CENTROIDS)


def setup_inputs(seed: int = 0) -> dict:
    streams_of = jax.random.split(jax.random.key(seed), 5)
    return {
        "features": draw_features(jax.random.fold_in(streams_of[4], 71), 0),
        "centroids": draw_centroids(jax.random.fold_in(streams_of[4], 71), 0),
        "row_weight": draw_row_weight(jax.random.fold_in(streams_of[4], 71), 0),
        "centroid_share": draw_centroid_share(jax.random.fold_in(streams_of[4], 71), 0),
    }


def reference(features, centroids, row_weight, centroid_share):
    feats = features.astype(jnp.float32)
    blocks = centroids.astype(jnp.float32).reshape(N_CENT, K_DEV, D)
    shares = centroid_share.reshape(N_CENT, K_DEV)

    def scores_of(block):
        return jnp.dot(feats, block.T, precision=lax.Precision.HIGHEST)

    row_max = jnp.max(lax.map(lambda block: jnp.max(scores_of(block), axis=1), blocks), axis=0)

    def kernel_of(block):
        return jnp.exp(scores_of(block) - row_max[:, None])

    def row_step(column_scale):
        def accumulate(running, pair):
            block, scale_part = pair
            return running + jnp.sum(kernel_of(block) * scale_part[None, :], axis=1), None

        running, unused = lax.scan(accumulate, jnp.zeros((ROWS,), jnp.float32), (blocks, column_scale))
        return row_weight / running

    def column_step(row_scale):
        def one_block(pair):
            block, share_part = pair
            return share_part / jnp.sum(kernel_of(block) * row_scale[:, None], axis=0)

        return lax.map(one_block, (blocks, shares))

    column_scale = jnp.ones((N_CENT, K_DEV), jnp.float32)
    for iteration in range(ITERS):
        row_scale = row_step(column_scale)
        column_scale = column_step(row_scale)
    row_scale = row_step(column_scale)

    def finish(pair):
        block, scale_part = pair
        transport = kernel_of(block) * row_scale[:, None] * scale_part[None, :]
        centroid_total = jnp.sum(transport, axis=0)
        weights = lax.optimization_barrier(transport.astype(jnp.bfloat16)).astype(jnp.float32)
        weighted = jnp.dot(feats.T, weights, precision=lax.Precision.HIGHEST)
        return weighted / centroid_total[None, :], centroid_total

    means_blocks, mass_blocks = lax.map(finish, (blocks, column_scale))
    centroid_means = jnp.transpose(means_blocks, (1, 0, 2)).reshape(D, CENTROIDS)
    return centroid_means, mass_blocks.reshape(CENTROIDS)
```

```python
import jax
import jax.numpy as jnp
from jax import lax
from jax.experimental import pallas as pl
from jax.experimental.pallas import tpu as pltpu
from jax.sharding import Mesh
from jax.sharding import PartitionSpec as P

ITERS = 3
ROWS = 1024
COLS = 2048
D = 1024
RB, CB = ROWS // 128, COLS // 128
CENT = ("z", "x")
DP = ("y", "core")
F32, BF16 = jnp.float32, jnp.bfloat16
VM = pl.BlockSpec(memory_space=pltpu.VMEM)
SM = pl.BlockSpec(memory_space=pltpu.SMEM)


def call(body, outs, ins, scratch=(), mib=24, name=None, aliases=None):
    return pl.pallas_call(
        body,
        out_shape=[jax.ShapeDtypeStruct(s, d) for s, d in outs],
        in_specs=[SM if a.dtype == jnp.int32 else VM for a in ins],
        out_specs=[VM] * len(outs),
        scratch_shapes=list(scratch),
        input_output_aliases=aliases or {},
        compiler_params=pltpu.CompilerParams(vmem_limit_bytes=mib << 20),
        name=name,
    )(*ins)


def step(x, axis, by):
    n = lax.axis_size(axis)
    return lax.ppermute(x, axis, [(i, (i + by) % n) for i in range(n)])


def everyone(x, axis):
    return lax.all_to_all(x, axis, 0, 0, tiled=True)


def down(row):
    return jnp.broadcast_to(row, (128, 128)).T


def strip_body(at_ref, a_ref, b_ref, c_ref, d_ref, o_ref):
    for k, ref in enumerate((a_ref, b_ref, c_ref, d_ref)):
        o_ref[pl.ds(pl.multiple_of(at_ref[k] * 32, 32), 32), :] = ref[...]


def score_body(at_ref, s_ref, r1, l1, r2, l2, r3, l3, h0, h1, c_ref, k_ref, ft_ref, fa_ref, p_ref):
    for k, ref in enumerate((s_ref, r1, l1, r2, l2, r3, l3)):
        ft_ref[at_ref[k]] = ref[...]
    ft_ref[at_ref[7], 0:64] = h0[...]
    ft_ref[at_ref[7], 64:128] = h1[...]
    for d in range(8):
        top = jnp.max(jnp.abs(ft_ref[d].astype(F32)), axis=0, keepdims=True)
        fa_ref[d : d + 1, :] = jnp.broadcast_to(jnp.max(top, axis=1, keepdims=True), (1, 128))
    for b in range(4):
        rows = slice(256 * b, 256 * b + 256)
        feats = ft_ref[:, :, rows].reshape(D, 256).T
        s = lax.dot_general(
            feats, c_ref[...], (((1,), (1,)), ((), ())), preferred_element_type=F32
        )
        k_ref[rows, :] = s
    for b in range(RB):
        rows = slice(128 * b, 128 * b + 128)
        s = k_ref[rows, :]
        top = jnp.max(s, axis=1, keepdims=True)
        e = jnp.exp(s - top)
        k_ref[rows, :] = e
        total = jnp.sum(e, axis=1, keepdims=True)
        p_ref[:, b : b + 1, :] = jnp.broadcast_to(
            jnp.broadcast_to(top, (128, 128)).T[0:1][None], (32, 1, 128)
        )
        p_ref[:, RB + b : RB + b + 1, :] = jnp.broadcast_to(
            jnp.broadcast_to(total, (128, 128)).T[0:1][None], (32, 1, 128)
        )


def columns(k_ref, scale, o_ref):
    acc = [jnp.zeros((8, 128), F32)] * CB
    for b in range(RB):
        rows = slice(128 * b, 128 * b + 128)
        by = down(scale[b : b + 1])
        for t in range(CB):
            part = k_ref[rows, 128 * t : 128 * t + 128] * by
            acc[t] = acc[t] + jnp.sum(part.reshape(16, 8, 128), axis=0)
    z = jnp.concatenate([jnp.sum(a, axis=0, keepdims=True) for a in acc], axis=0)
    o_ref[...] = jnp.broadcast_to(z[None], o_ref.shape)


def first_column_body(e_ref, mine_ref, a_ref, k_ref, o_ref, f_ref):
    peaks = e_ref[:, 0:RB, :]
    top = jnp.max(peaks, axis=0)
    total = jnp.sum(e_ref[:, RB : 2 * RB, :] * jnp.exp(peaks - top[None]), axis=0)
    fold = jnp.exp(mine_ref[0, 0:RB, :] - top)
    f_ref[...] = fold
    columns(k_ref, (a_ref[...] / total) * fold, o_ref)


def column_body(e_ref, f_ref, a_ref, k_ref, o_ref):
    scale = a_ref[...] / jnp.sum(e_ref[...], axis=0)
    columns(k_ref, scale * f_ref[...], o_ref)


def row_body(e_ref, f_ref, b_ref, k_ref, o_ref, c_ref):
    scale = b_ref[...] / jnp.sum(e_ref[...], axis=0)
    c_ref[...] = scale
    lines = []
    for b in range(RB):
        rows = slice(128 * b, 128 * b + 128)
        acc = jnp.zeros((128, 128), F32)
        for t in range(CB):
            acc = acc + k_ref[rows, 128 * t : 128 * t + 128] * scale[t : t + 1]
        lines.append(jnp.sum(acc.T, axis=0, keepdims=True))
    y = jnp.concatenate(lines, axis=0) * f_ref[...]
    o_ref[...] = jnp.broadcast_to(y[None], o_ref.shape)


def weight_body(e_ref, f_ref, a_ref, c_ref, fa_ref, k_ref, w_ref, m_ref):
    scale = (a_ref[...] / jnp.sum(e_ref[...], axis=0)) * f_ref[...]
    acc = [jnp.zeros((8, 128), F32)] * CB
    for b in range(RB):
        rows = slice(128 * b, 128 * b + 128)
        by = down(scale[b : b + 1])
        for t in range(CB):
            cols = slice(128 * t, 128 * t + 128)
            part = (k_ref[rows, cols] * by) * c_ref[t : t + 1, :]
            acc[t] = acc[t] + jnp.sum(part.reshape(16, 8, 128), axis=0)
            w_ref[rows, cols] = part.astype(BF16)
    m_ref[0:CB, :] = jnp.concatenate([jnp.sum(a, axis=0, keepdims=True) for a in acc], axis=0)
    m_ref[CB : CB + 8, :] = fa_ref[...]


def product_body(at_ref, ft_ref, w_ref, *o_refs):
    for k, o_ref in enumerate(o_refs):
        o_ref[...] = jnp.dot(ft_ref[at_ref[k]], w_ref[...], preferred_element_type=F32)


def per_device(features, centroids, row_weight, centroid_share):
    y, core, z, x = (lax.axis_index(n) for n in ("y", "core", "z", "x"))
    a = row_weight.reshape(RB, 128)
    share = centroid_share.reshape(CB, 128)

    own = features.T
    parts = [own] + [step(own, "x", k) for k in (1, 2, 3)]
    at = jnp.stack([(x - k) % 4 for k in range(4)]).astype(jnp.int32)
    (strip,) = call(strip_body, [((128, ROWS), BF16)], [at, *parts], mib=8, name="strip")
    right = left = strip
    ring = [strip]
    for _ in range(3):
        right, left = step(right, "z", 1), step(left, "z", -1)
        ring += [right, left]
    ring += [step(right[:64], "z", 1), step(left[64:], "z", -1)]
    at = jnp.stack([(z + k) % 8 for k in (0, -1, 1, -2, 2, -3, 3, 4)]).astype(jnp.int32)
    kernel, ft, fa, peaks = call(
        score_body,
        [((ROWS, COLS), F32), ((8, 128, ROWS), BF16), ((8, 128), F32), ((32, 2 * RB, 128), F32)],
        [at, *ring, centroids],
        mib=40,
        name="score",
    )
    got = everyone(peaks, CENT)
    sums, fold = call(
        first_column_body,
        [((8, CB, 128), F32), ((RB, 128), F32)],
        [got, peaks, a, kernel],
        name="column0",
    )
    for it in range(ITERS):
        rows, cscale = call(
            row_body,
            [((32, RB, 128), F32), ((CB, 128), F32)],
            [everyone(sums, DP), fold, share, kernel],
            name="row",
        )
        got = everyone(rows, CENT)
        if it < ITERS - 1:
            (sums,) = call(
                column_body, [((8, CB, 128), F32)], [got, fold, a, kernel], name="column"
            )
    weights, mass = call(
        weight_body,
        [((ROWS, COLS), BF16), ((CB + 8, 128), F32)],
        [got, fold, a, cscale, fa, kernel],
        name="weights",
    )

    other = step(mass, "core", 1)
    chip = jnp.concatenate([mass[:CB] + other[:CB], jnp.maximum(mass[CB:], other[CB:])], axis=0)
    chips = [chip] + [step(chip, "y", k) for k in (1, 2, 3)]

    def block(by, side):
        return 2 * ((y + by) % 4) + (core + side) % 2

    def limits(m, d):
        return (m[:CB] * lax.dynamic_slice(m, (CB + d, 0), (1, 128))).reshape(1, COLS)

    def products(which):
        at = jnp.stack([block(*w) for w in which]).astype(jnp.int32)
        return call(
            product_body,
            [((128, COLS), F32)] * len(which),
            [at, ft, weights],
            name="product",
        )

    def packed(mine, theirs, by):
        q = limits(chip, block(by, 0))
        inverse = jnp.where(q > 0, 32768.0 / q, 0.0)
        return ((mine + theirs) * inverse).astype(jnp.float16)

    sent = {}
    (give,) = products([(2, 1)])
    theirs = step(give, "core", 1)
    (mine,) = products([(2, 0)])
    sent[2] = step(packed(mine, theirs, 2), "y", 2)
    gives = products([(1, 1), (3, 1)])
    theirs = [step(g, "core", 1) for g in gives]
    mines = products([(1, 0), (3, 0)])
    sent[1] = step(packed(mines[0], theirs[0], 1), "y", 1)
    sent[3] = step(packed(mines[1], theirs[1], 3), "y", 3)
    give, mine = products([(0, 1), (0, 0)])
    total = mine + step(give, "core", 1)

    here = block(0, 0)
    for by in (1, 2, 3):
        total = total + sent[by].astype(F32) * (limits(chips[by], here) * (1.0 / 32768.0))
    centroid_total = (chips[0][:CB] + chips[2][:CB]) + (chips[1][:CB] + chips[3][:CB])
    return total / centroid_total.reshape(1, COLS), centroid_total.reshape(COLS)


def solution(mesh):
    split = Mesh(mesh.devices.reshape(4, 2, 8, 4), ("y", "core", "z", "x"))
    return jax.shard_map(
        per_device,
        mesh=split,
        in_specs=(P(DP, CENT), P(CENT, None), P(DP), P(CENT)),
        out_specs=(P(DP, CENT), P(CENT)),
        check_vma=False,
    )
```

```python
import functools

import jax
import jax.numpy as jnp
from jax import lax
from jax.experimental import pallas as pl
from jax.experimental.pallas import tpu as pltpu
from jax.sharding import Mesh
from jax.sharding import PartitionSpec as P

ITERS = 3
ROWS = 1024
COLS = 2048
RB, CB = ROWS // 128, COLS // 128
CENT = ("z", "x")
DP = ("y", "core")
F32, BF16 = jnp.float32, jnp.bfloat16
VM = pl.BlockSpec(memory_space=pltpu.VMEM)
SM = pl.BlockSpec(memory_space=pltpu.SMEM)


def call(body, outs, ins, scratch=(), mib=24, aliases=None):
    return pl.pallas_call(
        body,
        out_shape=[jax.ShapeDtypeStruct(s, d) for s, d in outs],
        in_specs=[SM if a.dtype == jnp.int32 else VM for a in ins],
        out_specs=[VM] * len(outs),
        scratch_shapes=list(scratch),
        input_output_aliases=aliases or {},
        compiler_params=pltpu.CompilerParams(vmem_limit_bytes=mib << 20),
    )(*ins)


def step(x, axis, by):
    n = lax.axis_size(axis)
    return lax.ppermute(x, axis, [(i, (i + by) % n) for i in range(n)])


def everyone(x, axis):
    return lax.all_to_all(x, axis, 0, 0, tiled=True)


def after(x, *others):
    return lax.optimization_barrier((x, *others))[0]


def down(row):
    return jnp.broadcast_to(row, (128, 128)).T


def around(at_ref, k, by, n):
    return lax.rem(at_ref[k] + (n + by), n)


def join_body(a_ref, b_ref, o_ref):
    o_ref[0:32, :] = a_ref[...]
    o_ref[32:64, :] = b_ref[...]


def collect(at_ref, pieces, c_ref, ft_ref, fa_ref, fs_ref, cs_ref):
    for k, (by, first, second) in enumerate(pieces):
        at = around(at_ref, 2, by, 8)
        for half, refs in ((0, first), (1, second)):
            for j, (ref, row) in enumerate(refs):
                x = around(at_ref, 3, (0, -1, 1, 2)[2 * half + j], 4)
                ft_ref[4 * at + x] = ref[row : row + 32, :]
        piece = ft_ref[pl.ds(4 * at, 4)].reshape(128, ROWS)
        top = jnp.max(jnp.abs(piece.astype(F32)), axis=0, keepdims=True)
        fa_ref[pl.ds(at, 1), :] = jnp.broadcast_to(jnp.max(top, axis=1, keepdims=True), (1, 128))
        fs_ref[:, 128 * k : 128 * k + 128] = piece.T
        cs_ref[:, 128 * k : 128 * k + 128] = c_ref[:, pl.ds(pl.multiple_of(at * 128, 128), 128)]


def product(f, c):
    return lax.dot_general(f, c, (((1,), (1,)), ((), ())), preferred_element_type=F32)


def whole(ref):
    return [(ref, 0), (ref, 32)]


def score0_body(at_ref, a0, b0, ar, br, al, bl, ar2, br2, c_ref, k_ref, ft_ref, fa_ref, fs, cs):
    pieces = [(0, whole(a0), whole(b0)), (-1, whole(ar), whole(br)), (1, whole(al), whole(bl))]
    pieces.append((-2, whole(ar2), whole(br2)))
    collect(at_ref, pieces, c_ref, ft_ref, fa_ref, fs, cs)

    def block(b, carry):
        rows = pl.ds(pl.multiple_of(256 * b, 256), 256)
        k_ref[rows, :] = product(fs[rows, :], cs[...])
        return carry

    lax.fori_loop(0, 4, block, 0)


def score1_body(at_ref, al2, bl2, ar3, br3, c_ref, kin, ftin, fain, k_ref, ft_ref, fa_ref, fs, cs):
    collect(
        at_ref,
        [(2, whole(al2), whole(bl2)), (-3, whole(ar3), whole(br3))],
        c_ref, ft_ref, fa_ref, fs, cs,
    )

    def block(b, carry):
        rows = pl.ds(pl.multiple_of(256 * b, 256), 256)
        k_ref[rows, :] = kin[rows, :] + product(fs[rows, :], cs[...])
        return carry

    lax.fori_loop(0, 4, block, 0)


def score2_body(
    at_ref, al3, bl3, ah0, ah1, bh0, bh1, c_ref, kin, ftin, fain, k_ref, ft_ref, fa_ref, p_ref, fs, cs
):
    far = (4, [(ah0, 0), (ah1, 0)], [(bh0, 0), (bh1, 0)])
    collect(at_ref, [(3, whole(al3), whole(bl3)), far], c_ref, ft_ref, fa_ref, fs, cs)

    def block(b, carry):
        rows = pl.ds(pl.multiple_of(128 * b, 128), 128)
        s = kin[rows, :] + product(fs[rows, :], cs[...])
        top = jnp.max(s, axis=1, keepdims=True)
        e = jnp.exp(s - top)
        k_ref[rows, :] = e
        total = jnp.sum(e, axis=1, keepdims=True)
        for k, v in ((0, top), (RB, total)):
            line = jnp.broadcast_to(v, (128, 128)).T[0:1][None]
            p_ref[:, pl.ds(k + b, 1), :] = jnp.broadcast_to(line, (32, 1, 128))
        return carry

    lax.fori_loop(0, RB, block, 0)


def columns(k_ref, scale, o_ref):
    acc = [jnp.zeros((8, 128), F32)] * CB
    for b in range(RB):
        rows = slice(128 * b, 128 * b + 128)
        by = down(scale[b : b + 1])
        for t in range(CB):
            part = k_ref[rows, 128 * t : 128 * t + 128] * by
            acc[t] = acc[t] + jnp.sum(part.reshape(16, 8, 128), axis=0)
    z = jnp.concatenate([jnp.sum(a, axis=0, keepdims=True) for a in acc], axis=0)
    o_ref[...] = jnp.broadcast_to(z[None], o_ref.shape)


def first_column_body(e_ref, mine_ref, a_ref, k_ref, o_ref, f_ref):
    peaks = e_ref[:, 0:RB, :]
    top = jnp.max(peaks, axis=0)
    total = jnp.sum(e_ref[:, RB : 2 * RB, :] * jnp.exp(peaks - top[None]), axis=0)
    fold = jnp.exp(mine_ref[0, 0:RB, :] - top)
    f_ref[...] = fold
    columns(k_ref, (a_ref[...] / total) * fold, o_ref)


def column_body(e_ref, f_ref, a_ref, k_ref, o_ref):
    scale = a_ref[...] / jnp.sum(e_ref[...], axis=0)
    columns(k_ref, scale * f_ref[...], o_ref)


def row_body(e_ref, f_ref, b_ref, k_ref, o_ref, c_ref):
    scale = b_ref[...] / jnp.sum(e_ref[...], axis=0)
    c_ref[...] = scale
    lines = []
    for b in range(RB):
        rows = slice(128 * b, 128 * b + 128)
        acc = jnp.zeros((128, 128), F32)
        for t in range(CB):
            acc = acc + k_ref[rows, 128 * t : 128 * t + 128] * scale[t : t + 1]
        lines.append(jnp.sum(acc.T, axis=0, keepdims=True))
    y = jnp.concatenate(lines, axis=0) * f_ref[...]
    o_ref[...] = jnp.broadcast_to(y[None], o_ref.shape)


def target(at_ref, by, side):
    return 2 * around(at_ref, 0, by, 4) + around(at_ref, 1, side, 2)


def product_of(at_ref, ft_ref, w_ref, o_ref, by, side):
    d = 4 * target(at_ref, by, side)

    def block(b, carry):
        cols = pl.ds(pl.multiple_of(512 * b, 512), 512)
        feats = ft_ref[pl.ds(d, 4)].reshape(128, ROWS)
        o_ref[:, cols] = jnp.dot(feats, w_ref[:, cols], preferred_element_type=F32)
        return carry

    lax.fori_loop(0, COLS // 512, block, 0)


def weight_body(
    at_ref, e_ref, f_ref, a_ref, c_ref, fa_ref, k_ref, ft_ref, w_ref, m_ref, o_ref
):
    scale = (a_ref[...] / jnp.sum(e_ref[...], axis=0)) * f_ref[...]
    acc = [jnp.zeros((8, 128), F32)] * CB
    for b in range(RB):
        rows = slice(128 * b, 128 * b + 128)
        by = down(scale[b : b + 1])
        for t in range(CB):
            cols = slice(128 * t, 128 * t + 128)
            part = (k_ref[rows, cols] * by) * c_ref[t : t + 1, :]
            acc[t] = acc[t] + jnp.sum(part.reshape(16, 8, 128), axis=0)
            w_ref[rows, cols] = part.astype(BF16)
    m_ref[0:CB, :] = jnp.concatenate([jnp.sum(a, axis=0, keepdims=True) for a in acc], axis=0)
    m_ref[CB : CB + 8, :] = fa_ref[...]
    product_of(at_ref, ft_ref, w_ref, o_ref, 2, 1)


def limits(at_ref, m, by):
    return m[0:CB, :] * m[pl.ds(CB + target(at_ref, by, 0), 1), :]


def chip_body(at_ref, mine_ref, other_ref, m_ref, i_ref):
    m_ref[0:CB, :] = mine_ref[0:CB, :] + other_ref[0:CB, :]
    m_ref[CB : CB + 8, :] = jnp.maximum(mine_ref[CB : CB + 8, :], other_ref[CB : CB + 8, :])
    for k, by in enumerate((2, 1, 3)):
        q = limits(at_ref, m_ref, by)
        i_ref[k] = jnp.where(q > 0, 32768.0 / jnp.where(q > 0, q, 1.0), 0.0)


def share_body(at_ref, m0, m1, m2, m3, t_ref, i_ref, s_ref):
    total = (m0[0:CB, :] + m2[0:CB, :]) + (m1[0:CB, :] + m3[0:CB, :])
    t_ref[...] = total
    i_ref[...] = 1.0 / total
    for k, m in enumerate((m2, m1, m3)):
        s_ref[k] = (limits(at_ref, m, 0) * (1.0 / 32768.0)) / total


def product_body(which, at_ref, ft_ref, w_ref, *o_refs):
    for k, o_ref in enumerate(o_refs):
        product_of(at_ref, ft_ref, w_ref, o_ref, *which[k])


def assigned(features, centroids, row_weight, centroid_share):
    y, core, z, x = (lax.axis_index(n) for n in ("y", "core", "z", "x"))
    at = jnp.stack([y, core, z, x]).astype(jnp.int32)
    a = row_weight.reshape(RB, 128)
    share = centroid_share.reshape(CB, 128)

    own = after(features.T, at)
    (half_a,) = call(join_body, [((64, ROWS), BF16)], [own, step(own, "x", 1)], mib=4)
    (half_b,) = call(
        join_body, [((64, ROWS), BF16)], [step(own, "x", -1), step(own, "x", 2)], mib=4
    )
    right, left = {0: [half_a, half_b]}, {0: [half_a, half_b]}
    for k in (1, 2, 3):
        right[k] = [step(h, "z", 1) for h in right[k - 1]]
        left[k] = [step(h, "z", -1) for h in left[k - 1]]
    state = [((ROWS, COLS), F32), ((32, 32, ROWS), BF16), ((8, 128), F32)]
    kernel, ft, fa = call(
        score0_body,
        state,
        [at, *right[0], *right[1], *left[1], *right[2], centroids],
        scratch=[pltpu.VMEM((ROWS, 512), BF16), pltpu.VMEM((COLS, 512), BF16)],
        mib=16,
    )
    far = []
    for h in (0, 1):
        far += [step(after(right[3][h], fa)[:32], "z", 1), step(after(left[3][h], fa)[32:], "z", -1)]
    two = [pltpu.VMEM((ROWS, 256), BF16), pltpu.VMEM((COLS, 256), BF16)]
    kernel, ft, fa = call(
        score1_body,
        state,
        [at, *left[2], *right[3], centroids, kernel, ft, fa],
        scratch=two,
        mib=16,
        aliases={6: 0, 7: 1, 8: 2},
    )
    kernel, ft, fa, peaks = call(
        score2_body,
        [*state, ((32, 2 * RB, 128), F32)],
        [at, *left[3], *far, centroids, kernel, ft, fa],
        scratch=two,
        mib=16,
        aliases={8: 0, 9: 1, 10: 2},
    )
    got = everyone(peaks, CENT)
    sums, fold = call(
        first_column_body, [((8, CB, 128), F32), ((RB, 128), F32)], [got, peaks, a, kernel], mib=8
    )
    for it in range(ITERS):
        rows, cscale = call(
            row_body,
            [((32, RB, 128), F32), ((CB, 128), F32)],
            [everyone(sums, DP), fold, share, kernel],
            mib=8,
        )
        got = everyone(rows, CENT)
        if it < ITERS - 1:
            (sums,) = call(column_body, [((8, CB, 128), F32)], [got, fold, a, kernel], mib=8)
    weights, mass, give = call(
        weight_body,
        [((ROWS, COLS), BF16), ((CB + 8, 128), F32), ((128, COLS), F32)],
        [at, got, fold, a, cscale, fa, kernel, ft],
        mib=16,
    )

    chip, inverse = call(
        chip_body,
        [((CB + 8, 128), F32), ((3, CB, 128), F32)],
        [at, mass, step(mass, "core", 1)],
        mib=4,
    )
    inverse = inverse.reshape(3, 1, COLS)

    def products(which, where):
        return call(
            functools.partial(product_body, which),
            [((128, COLS), F32)] * len(which),
            [where, ft, weights],
            mib=16,
        )

    def send(x, by):
        return step(x, "y", by)

    def packed(mine, theirs, k):
        return ((mine + theirs) * inverse[k]).astype(jnp.float16)

    theirs = step(give, "core", 1)
    (mine,) = products([(2, 0)], at)
    ready = packed(mine, theirs, 0)
    sent = [send(ready, 2)]
    gives = products([(1, 1), (3, 1)], after(at, ready))
    theirs = [step(g, "core", 1) for g in gives]
    mines = products([(1, 0), (3, 0)], after(at, *gives))
    ready = [packed(m, t, k) for m, t, k in zip(mines, theirs, (1, 2))]
    sent += [send(ready[0], 1), send(ready[1], 3)]
    give, mine = products([(0, 1), (0, 0)], after(at, *ready))
    theirs = step(give, "core", 1)
    chip = after(chip, *ready)
    total, over, shares = call(
        share_body,
        [((CB, 128), F32), ((CB, 128), F32), ((3, CB, 128), F32)],
        [at, chip, *(step(chip, "y", k) for k in (1, 2, 3))],
        mib=4,
    )
    shares = shares.reshape(3, 1, COLS)
    means = (mine + theirs) * over.reshape(1, COLS)
    for k in range(3):
        means = means + sent[k].astype(F32) * shares[k]
    return means, total.reshape(COLS)


def solution(mesh):
    split = Mesh(mesh.devices.reshape(4, 2, 8, 4), ("y", "core", "z", "x"))
    return jax.shard_map(
        assigned,
        mesh=split,
        in_specs=(P(DP, CENT), P(CENT, None), P(DP), P(CENT)),
        out_specs=(P(DP, CENT), P(CENT)),
        check_vma=False,
    )
```

```python
import functools

import jax
import jax.numpy as jnp
from jax import lax
from jax.experimental import pallas as pl
from jax.experimental.pallas import tpu as pltpu
from jax.sharding import Mesh
from jax.sharding import PartitionSpec as P

ITERS = 3
ROWS = 1024
COLS = 2048
RB, CB = ROWS // 128, COLS // 128
CENT = ("z", "x")
DP = ("y", "core")
F32, BF16 = jnp.float32, jnp.bfloat16
VM = pl.BlockSpec(memory_space=pltpu.VMEM)
SM = pl.BlockSpec(memory_space=pltpu.SMEM)


def call(body, outs, ins, scratch=(), mib=24, aliases=None):
    return pl.pallas_call(
        body,
        out_shape=[jax.ShapeDtypeStruct(s, d) for s, d in outs],
        in_specs=[SM if a.dtype == jnp.int32 else VM for a in ins],
        out_specs=[VM] * len(outs),
        scratch_shapes=list(scratch),
        input_output_aliases=aliases or {},
        compiler_params=pltpu.CompilerParams(vmem_limit_bytes=mib << 20),
    )(*ins)


def step(x, axis, by):
    n = lax.axis_size(axis)
    return lax.ppermute(x, axis, [(i, (i + by) % n) for i in range(n)])


def everyone(x, axis):
    return lax.all_to_all(x, axis, 0, 0, tiled=True)


def after(x, *others):
    return lax.optimization_barrier((x, *others))[0]


def down(row):
    return jnp.broadcast_to(row, (128, 128)).T


def around(at_ref, k, by, n):
    return lax.rem(at_ref[k] + (n + by), n)


def own_body(a_ref, o_ref):
    o_ref[0:32, :] = a_ref[...]


def join_body(b_ref, c_ref, d_ref, in_ref, o_ref):
    for k, ref in enumerate((b_ref, c_ref, d_ref)):
        o_ref[32 * k + 32 : 32 * k + 64, :] = ref[...]


def collect(at_ref, pieces, c_ref, ft_ref, fa_ref, fs_ref, cs_ref):
    for k, (by, parts) in enumerate(pieces):
        at = around(at_ref, 2, by, 8)
        for (ref, row), off in zip(parts, (0, -1, 1, 2)):
            ft_ref[4 * at + around(at_ref, 3, off, 4)] = ref[row : row + 32, :]
        piece = ft_ref[pl.ds(4 * at, 4)].reshape(128, ROWS)
        top = jnp.max(jnp.abs(piece), axis=0, keepdims=True).astype(F32)
        fa_ref[pl.ds(at, 1), :] = jnp.broadcast_to(jnp.max(top, axis=1, keepdims=True), (1, 128))
        fs_ref[:, 128 * k : 128 * k + 128] = piece.T
        cs_ref[:, 128 * k : 128 * k + 128] = c_ref[:, pl.ds(pl.multiple_of(at * 128, 128), 128)]


def product(f, c):
    return lax.dot_general(f, c, (((1,), (1,)), ((), ())), preferred_element_type=F32)


def whole(ref):
    return [(ref, 32 * k) for k in range(4)]


def accumulate(kin, k_ref, fs, cs):
    def block(b, carry):
        rows = pl.ds(pl.multiple_of(256 * b, 256), 256)
        s = product(fs[rows, :], cs[...])
        k_ref[rows, :] = s if kin is None else kin[rows, :] + s
        return carry

    lax.fori_loop(0, 4, block, 0)


def score0_body(at_ref, s_ref, c_ref, k_ref, ft_ref, fa_ref, fs, cs):
    collect(at_ref, [(0, whole(s_ref))], c_ref, ft_ref, fa_ref, fs, cs)
    accumulate(None, k_ref, fs, cs)


def score_body(by, at_ref, l, r, c_ref, kin, ftin, fain, k_ref, ft_ref, fa_ref, fs, cs):
    collect(at_ref, [(by, whole(l)), (-by, whole(r))], c_ref, ft_ref, fa_ref, fs, cs)
    accumulate(kin, k_ref, fs, cs)


def score4_body(at_ref, h0, h1, c_ref, kin, ftin, fain, k_ref, ft_ref, fa_ref, p_ref, fs, cs, tops, sums):
    far = (4, [(h0, 0), (h0, 32), (h1, 0), (h1, 32)])
    collect(at_ref, [far], c_ref, ft_ref, fa_ref, fs, cs)

    def scored(b):
        rows = pl.ds(pl.multiple_of(128 * b, 128), 128)
        s = kin[rows, :] + product(fs[rows, :], cs[...])
        k_ref[rows, :] = s
        tops[rows, :] = jnp.broadcast_to(jnp.max(s, axis=1, keepdims=True), (128, 128))

    def raised(b):
        rows = pl.ds(pl.multiple_of(128 * b, 128), 128)
        top, acc = tops[rows, :], jnp.zeros((128, 128), F32)
        for t in range(CB):
            cols = slice(128 * t, 128 * t + 128)
            e = jnp.exp(k_ref[rows, cols] - top)
            k_ref[rows, cols] = e
            acc = acc + e
        sums[rows, :] = acc

    def block(b, carry):
        raised(b)
        scored(b + 1)
        return carry

    scored(0)
    lax.fori_loop(0, RB - 1, block, 0)
    raised(RB - 1)
    lines = [tops[128 * b : 128 * b + 128, :].T[0:1] for b in range(RB)]
    lines += [jnp.sum(sums[128 * b : 128 * b + 128, :].T, axis=0, keepdims=True) for b in range(RB)]
    p_ref[...] = jnp.broadcast_to(jnp.concatenate(lines, axis=0)[None], p_ref.shape)


def columns(k_ref, scale, by_ref, o_ref):
    for b in range(RB):
        by_ref[128 * b : 128 * b + 128, :] = down(scale[b : b + 1])

    def block(b, acc):
        rows = pl.ds(pl.multiple_of(128 * b, 128), 128)
        by = by_ref[rows, :]
        parts = (k_ref[rows, 128 * t : 128 * t + 128] * by for t in range(CB))
        return tuple(a + jnp.sum(p.reshape(16, 8, 128), axis=0) for a, p in zip(acc, parts))

    acc = lax.fori_loop(0, RB, block, (jnp.zeros((8, 128), F32),) * CB)
    z = jnp.concatenate([jnp.sum(a, axis=0, keepdims=True) for a in acc], axis=0)
    o_ref[...] = jnp.broadcast_to(z[None], o_ref.shape)


def first_column_body(e_ref, mine_ref, a_ref, k_ref, o_ref, f_ref, by_ref):
    peaks = e_ref[:, 0:RB, :]
    top = jnp.max(peaks, axis=0)
    total = jnp.sum(e_ref[:, RB : 2 * RB, :] * jnp.exp(peaks - top[None]), axis=0)
    fold = jnp.exp(mine_ref[0, 0:RB, :] - top)
    f_ref[...] = fold
    columns(k_ref, (a_ref[...] / total) * fold, by_ref, o_ref)


def column_body(e_ref, f_ref, a_ref, k_ref, o_ref, by_ref):
    scale = a_ref[...] / jnp.sum(e_ref[...], axis=0)
    columns(k_ref, scale * f_ref[...], by_ref, o_ref)


def row_body(e_ref, f_ref, b_ref, k_ref, o_ref, c_ref, acc_ref):
    scale = b_ref[...] / jnp.sum(e_ref[...], axis=0)
    c_ref[...] = scale

    def block(b, carry):
        rows = pl.ds(pl.multiple_of(128 * b, 128), 128)
        acc = jnp.zeros((128, 128), F32)
        for t in range(CB):
            acc = acc + k_ref[rows, 128 * t : 128 * t + 128] * scale[t : t + 1]
        acc_ref[rows, :] = acc
        return carry

    lax.fori_loop(0, RB, block, 0)
    lines = [
        jnp.sum(acc_ref[128 * b : 128 * b + 128, :].T, axis=0, keepdims=True) for b in range(RB)
    ]
    y = jnp.concatenate(lines, axis=0) * f_ref[...]
    o_ref[...] = jnp.broadcast_to(y[None], o_ref.shape)


def target(at_ref, by, side):
    return 2 * around(at_ref, 0, by, 4) + around(at_ref, 1, side, 2)


def product_of(at_ref, ft_ref, w_ref, o_ref, by, side):
    feats = ft_ref[pl.ds(4 * target(at_ref, by, side), 4)].reshape(128, ROWS)
    o_ref[...] = jnp.dot(feats, w_ref[...], preferred_element_type=F32)


def halves_of(at_ref, ft_ref, w_ref, o_ref, by, side):
    d = 4 * target(at_ref, by, side)

    def block(b, carry):
        cols = pl.ds(pl.multiple_of(1024 * b, 1024), 1024)
        feats = ft_ref[pl.ds(d, 4)].reshape(128, ROWS)
        o_ref[:, cols] = jnp.dot(feats, w_ref[:, cols], preferred_element_type=F32)
        return carry

    lax.fori_loop(0, 2, block, 0)


def weight_body(e_ref, f_ref, a_ref, c_ref, fa_ref, k_ref, w_ref, m_ref, by_ref):
    scale = (a_ref[...] / jnp.sum(e_ref[...], axis=0)) * f_ref[...]
    for b in range(RB):
        by_ref[128 * b : 128 * b + 128, :] = down(scale[b : b + 1])

    def block(b, acc):
        rows = pl.ds(pl.multiple_of(128 * b, 128), 128)
        by, total = by_ref[rows, :], []
        for t in range(CB):
            cols = slice(128 * t, 128 * t + 128)
            part = (k_ref[rows, cols] * by) * c_ref[t : t + 1, :]
            total.append(acc[t] + jnp.sum(part.reshape(16, 8, 128), axis=0))
            w_ref[rows, cols] = part.astype(BF16)
        return tuple(total)

    acc = lax.fori_loop(0, RB, block, (jnp.zeros((8, 128), F32),) * CB)
    m_ref[0:CB, :] = jnp.concatenate([jnp.sum(a, axis=0, keepdims=True) for a in acc], axis=0)
    m_ref[CB : CB + 8, :] = fa_ref[...]


def limits(at_ref, m, by):
    return m[0:CB, :] * m[pl.ds(CB + target(at_ref, by, 0), 1), :]


def inverse(q):
    return jnp.where(q > 0, 32768.0 / jnp.where(q > 0, q, 1.0), 0.0)


def chip_body(at_ref, mine_ref, other_ref, m_ref, i_ref):
    m_ref[0:CB, :] = mine_ref[0:CB, :] + other_ref[0:CB, :]
    m_ref[CB : CB + 8, :] = jnp.maximum(mine_ref[CB : CB + 8, :], other_ref[CB : CB + 8, :])
    for k, by in enumerate((2, 1, 3)):
        i_ref[k] = inverse(limits(at_ref, m_ref, by))


def relay_body(at_ref, m0, m1, m3, i_ref, s_ref):
    for k, (m, by) in enumerate(((m1, 1), (m3, 3))):
        q = limits(at_ref, m, by)
        s_ref[k] = q * (1.0 / 32768.0)
        i_ref[k] = inverse(q + limits(at_ref, m0, by))


def share_body(at_ref, m0, m1, m2, m3, t_ref, i_ref, s_ref):
    total = (m0[0:CB, :] + m2[0:CB, :]) + (m1[0:CB, :] + m3[0:CB, :])
    t_ref[...] = total
    over = 1.0 / total
    i_ref[...] = over
    q1, q2, q3 = (limits(at_ref, m, 0) * (1.0 / 32768.0) for m in (m1, m2, m3))
    for k, q in enumerate((q1, q3, q1 + q2, q3 + q2)):
        s_ref[k] = q * over


def product_body(which, at_ref, ft_ref, w_ref, *o_refs):
    one = product_of if len(which) == 1 else halves_of
    for k, o_ref in enumerate(o_refs):
        one(at_ref, ft_ref, w_ref, o_ref, *which[k])


def assigned(features, centroids, row_weight, centroid_share):
    y, core, z, x = (lax.axis_index(n) for n in ("y", "core", "z", "x"))
    at = jnp.stack([y, core, z, x]).astype(jnp.int32)
    a = row_weight.reshape(RB, 128)
    share = centroid_share.reshape(CB, 128)

    own = after(features.T, at)

    def ring(x, by):
        return step(x, "z", by)

    def scores(body, outs, ins, depth, aliases=None, more=()):
        return call(
            body,
            outs,
            ins,
            scratch=[pltpu.VMEM((ROWS, depth), BF16), pltpu.VMEM((COLS, depth), BF16), *more],
            mib=16,
            aliases=aliases,
        )

    parts = []
    for by in (1, -1, 2):
        parts.append(step(own, "x", by))
    strip_shape = [((128, ROWS), BF16)]
    (strip,) = call(own_body, strip_shape, [own], mib=4)
    (strip,) = call(join_body, strip_shape, [*parts, strip], mib=4, aliases={3: 0})
    state = [((ROWS, COLS), F32), ((32, 32, ROWS), BF16), ((8, 128), F32)]
    right = [strip, ring(strip, 1)]
    left = [strip, ring(strip, -1)]
    kernel, ft, fa = scores(score0_body, state, [at, strip, centroids], 128)
    for k in (1, 2):
        right.append(ring(right[k], 1))
        left.append(ring(left[k], -1))
    far = [ring(right[3][:64], 1), ring(left[3][64:], -1)]
    for k in (1, 2, 3):
        kernel, ft, fa = scores(
            functools.partial(score_body, k),
            state,
            [at, left[k], right[k], centroids, kernel, ft, fa],
            256,
            {4: 0, 5: 1, 6: 2},
        )
    kernel, ft, fa, peaks = scores(
        score4_body,
        [*state, ((32, 2 * RB, 128), F32)],
        [at, *far, centroids, kernel, ft, fa],
        128,
        {4: 0, 5: 1, 6: 2},
        [pltpu.VMEM((ROWS, 128), F32)] * 2,
    )
    lines = [pltpu.VMEM((ROWS, 128), F32)]
    got = everyone(peaks, CENT)
    sums, fold = call(
        first_column_body,
        [((8, CB, 128), F32), ((RB, 128), F32)],
        [got, peaks, a, kernel],
        scratch=lines,
        mib=8,
    )
    for it in range(ITERS):
        rows, cscale = call(
            row_body,
            [((32, RB, 128), F32), ((CB, 128), F32)],
            [everyone(sums, DP), fold, share, kernel],
            scratch=lines,
            mib=8,
        )
        got = everyone(rows, CENT)
        if it < ITERS - 1:
            (sums,) = call(
                column_body, [((8, CB, 128), F32)], [got, fold, a, kernel], scratch=lines, mib=8
            )
    weights, mass = call(
        weight_body,
        [((ROWS, COLS), BF16), ((CB + 8, 128), F32)],
        [got, fold, a, cscale, fa, kernel],
        scratch=lines,
        mib=8,
    )

    other = step(mass, "core", 1)
    chip, packs = call(
        chip_body, [((CB + 8, 128), F32), ((3, CB, 128), F32)], [at, mass, other], mib=4
    )
    packs = packs.reshape(3, 1, COLS)

    def products(which, where):
        return call(
            functools.partial(product_body, which),
            [((128, COLS), F32)] * len(which),
            [where, ft, weights],
            mib=16,
        )

    def send(x, by):
        return step(x.astype(jnp.float16), "y", by)

    low, high = slice(0, 64), slice(64, 128)
    (give,) = products([(2, 1)], at)
    theirs = step(give, "core", 1)
    (mine,) = products([(2, 0)], after(at, give))
    chips = {}
    for by in (1, 3, 2):
        chips[by] = step(chip, "y", by)
    up = ((mine[low] + theirs[low]) * packs[0]).astype(jnp.float16)
    down_ = ((mine[high] + theirs[high]) * packs[0]).astype(jnp.float16)
    first = (send(up, 1), send(down_, 3))
    gives = products([(1, 1), (3, 1)], after(at, up, down_))
    theirs = [step(g, "core", 1) for g in gives]
    mines = products([(1, 0), (3, 0)], after(at, *gives))
    up = ((mines[0][high] + theirs[0][high]) * packs[1]).astype(jnp.float16)
    down_ = ((mines[1][low] + theirs[1][low]) * packs[2]).astype(jnp.float16)
    second = (send(up, 1), send(down_, 3))
    repacks, unpacks = call(
        relay_body, [((2, CB, 128), F32)] * 2, [at, chip, chips[1], chips[3]], mib=4
    )
    repacks, unpacks = repacks.reshape(2, 1, COLS), unpacks.reshape(2, 1, COLS)
    give, mine0 = products([(0, 1), (0, 0)], at)
    theirs0 = step(give, "core", 1)
    total, over, shares = call(
        share_body,
        [((CB, 128), F32), ((CB, 128), F32), ((4, CB, 128), F32)],
        [at, chip, chips[1], chips[2], chips[3]],
        mib=4,
    )
    mines, theirs, *_ = lax.optimization_barrier((mines, theirs, up, down_))
    up = mines[0][low] + theirs[0][low] + first[0].astype(F32) * unpacks[0]
    down_ = mines[1][high] + theirs[1][high] + first[1].astype(F32) * unpacks[1]
    third = (send(up * repacks[0], 1), send(down_ * repacks[1], 3))

    over, shares = over.reshape(1, COLS), shares.reshape(4, 1, COLS)
    own_part = (mine0 + theirs0) * over
    top = own_part[low] + second[1].astype(F32) * shares[1] + third[0].astype(F32) * shares[2]
    bottom = own_part[high] + second[0].astype(F32) * shares[0] + third[1].astype(F32) * shares[3]
    return jnp.concatenate([top, bottom], axis=0), total.reshape(COLS)


def solution(mesh):
    split = Mesh(mesh.devices.reshape(4, 2, 8, 4), ("y", "core", "z", "x"))
    return jax.shard_map(
        assigned,
        mesh=split,
        in_specs=(P(DP, CENT), P(CENT, None), P(DP), P(CENT)),
        out_specs=(P(DP, CENT), P(CENT)),
        check_vma=False,
    )
```

```python
import functools

import jax
import jax.numpy as jnp
from jax import lax
from jax.experimental import pallas as pl
from jax.experimental.pallas import tpu as pltpu
from jax.sharding import Mesh
from jax.sharding import PartitionSpec as P

ITERS = 3
ROWS = 1024
COLS = 2048
RB, CB = ROWS // 128, COLS // 128
CENT = ("z", "x")
DP = ("y", "core")
F32, BF16 = jnp.float32, jnp.bfloat16
VM = pl.BlockSpec(memory_space=pltpu.VMEM)
SM = pl.BlockSpec(memory_space=pltpu.SMEM)


def call(body, outs, ins, scratch=(), mib=24, aliases=None):
    return pl.pallas_call(
        body,
        out_shape=[jax.ShapeDtypeStruct(s, d) for s, d in outs],
        in_specs=[SM if a.dtype == jnp.int32 else VM for a in ins],
        out_specs=[VM] * len(outs),
        scratch_shapes=list(scratch),
        input_output_aliases=aliases or {},
        compiler_params=pltpu.CompilerParams(vmem_limit_bytes=mib << 20),
    )(*ins)


def step(x, axis, by):
    n = lax.axis_size(axis)
    return lax.ppermute(x, axis, [(i, (i + by) % n) for i in range(n)])


def everyone(x, axis):
    return lax.all_to_all(x, axis, 0, 0, tiled=True)


def after(x, *others):
    return lax.optimization_barrier((x, *others))[0]


def down(row):
    return jnp.broadcast_to(row, (128, 128)).T


def around(at_ref, k, by, n):
    return lax.rem(at_ref[k] + (n + by), n)


def own_body(a_ref, o_ref):
    o_ref[0:32, :] = a_ref[...]


def join_body(b_ref, c_ref, d_ref, in_ref, o_ref):
    for k, ref in enumerate((b_ref, c_ref, d_ref)):
        o_ref[32 * k + 32 : 32 * k + 64, :] = ref[...]


def collect(at_ref, pieces, c_ref, ft_ref, fa_ref, fs_ref, cs_ref):
    for k, (by, parts) in enumerate(pieces):
        at = around(at_ref, 2, by, 8)
        for (ref, row), off in zip(parts, (0, -1, 1, 2)):
            place = pl.multiple_of(32 * around(at_ref, 3, off, 4), 32)
            ft_ref[at, pl.ds(place, 32), :] = ref[row : row + 32, :]
        piece = ft_ref[at]
        top = jnp.max(jnp.abs(piece), axis=0, keepdims=True).astype(F32)
        fa_ref[pl.ds(at, 1), :] = jnp.broadcast_to(jnp.max(top, axis=1, keepdims=True), (1, 128))
        fs_ref[:, 128 * k : 128 * k + 128] = piece.T
        cs_ref[:, 128 * k : 128 * k + 128] = c_ref[:, pl.ds(pl.multiple_of(at * 128, 128), 128)]


def product(f, c):
    return lax.dot_general(f, c, (((1,), (1,)), ((), ())), preferred_element_type=F32)


def whole(ref):
    return [(ref, 32 * k) for k in range(4)]


def accumulate(kin, k_ref, fs, cs):
    def block(b, carry):
        rows = pl.ds(pl.multiple_of(256 * b, 256), 256)
        s = product(fs[rows, :], cs[...])
        k_ref[rows, :] = s if kin is None else kin[rows, :] + s
        return carry

    lax.fori_loop(0, 4, block, 0)


def score0_body(at_ref, s_ref, c_ref, k_ref, ft_ref, fa_ref, fs, cs):
    collect(at_ref, [(0, whole(s_ref))], c_ref, ft_ref, fa_ref, fs, cs)
    accumulate(None, k_ref, fs, cs)


def score_body(by, at_ref, l, r, c_ref, kin, ftin, fain, k_ref, ft_ref, fa_ref, fs, cs):
    collect(at_ref, [(by, whole(l)), (-by, whole(r))], c_ref, ft_ref, fa_ref, fs, cs)
    accumulate(kin, k_ref, fs, cs)


def score4_body(at_ref, h0, h1, c_ref, kin, ftin, fain, k_ref, ft_ref, fa_ref, p_ref, fs, cs, tops, sums):
    far = (4, [(h0, 0), (h0, 32), (h1, 0), (h1, 32)])
    collect(at_ref, [far], c_ref, ft_ref, fa_ref, fs, cs)

    def scored(b):
        rows = pl.ds(pl.multiple_of(128 * b, 128), 128)
        s = kin[rows, :] + product(fs[rows, :], cs[...])
        k_ref[rows, :] = s
        tops[rows, :] = jnp.broadcast_to(jnp.max(s, axis=1, keepdims=True), (128, 128))

    def raised(b):
        rows = pl.ds(pl.multiple_of(128 * b, 128), 128)
        top, acc = tops[rows, :], jnp.zeros((128, 128), F32)
        for t in range(CB):
            cols = slice(128 * t, 128 * t + 128)
            e = jnp.exp(k_ref[rows, cols] - top)
            k_ref[rows, cols] = e
            acc = acc + e
        sums[rows, :] = acc

    def block(b, carry):
        raised(b)
        scored(b + 1)
        return carry

    scored(0)
    lax.fori_loop(0, RB - 1, block, 0)
    raised(RB - 1)
    lines = [tops[128 * b : 128 * b + 128, :].T[0:1] for b in range(RB)]
    lines += [jnp.sum(sums[128 * b : 128 * b + 128, :].T, axis=0, keepdims=True) for b in range(RB)]
    p_ref[...] = jnp.broadcast_to(jnp.concatenate(lines, axis=0)[None], p_ref.shape)


def columns(k_ref, scale, o_ref):
    acc = [jnp.zeros((8, 128), F32)] * CB
    for b in range(RB):
        rows = slice(128 * b, 128 * b + 128)
        by = down(scale[b : b + 1])
        for t in range(CB):
            part = k_ref[rows, 128 * t : 128 * t + 128] * by
            acc[t] = acc[t] + jnp.sum(part.reshape(16, 8, 128), axis=0)
    z = jnp.concatenate([jnp.sum(a, axis=0, keepdims=True) for a in acc], axis=0)
    o_ref[...] = jnp.broadcast_to(z[None], o_ref.shape)


def first_column_body(e_ref, mine_ref, a_ref, k_ref, o_ref, f_ref):
    peaks = e_ref[:, 0:RB, :]
    top = jnp.max(peaks, axis=0)
    total = jnp.sum(e_ref[:, RB : 2 * RB, :] * jnp.exp(peaks - top[None]), axis=0)
    fold = jnp.exp(mine_ref[0, 0:RB, :] - top)
    f_ref[...] = fold
    columns(k_ref, (a_ref[...] / total) * fold, o_ref)


def column_body(e_ref, f_ref, a_ref, k_ref, o_ref):
    scale = a_ref[...] / jnp.sum(e_ref[...], axis=0)
    columns(k_ref, scale * f_ref[...], o_ref)


def row_body(e_ref, f_ref, b_ref, k_ref, o_ref, *refs):
    scale = b_ref[...] / jnp.sum(e_ref[...], axis=0)
    acc_ref = refs[-1]
    if len(refs) > 1:
        refs[0][...] = scale

    def block(b, carry):
        rows = pl.ds(pl.multiple_of(128 * b, 128), 128)
        acc = jnp.zeros((128, 128), F32)
        for t in range(CB):
            acc = acc + k_ref[rows, 128 * t : 128 * t + 128] * scale[t : t + 1]
        acc_ref[rows, :] = acc
        return carry

    lax.fori_loop(0, RB, block, 0)
    lines = [
        jnp.sum(acc_ref[128 * b : 128 * b + 128, :].T, axis=0, keepdims=True) for b in range(RB)
    ]
    y = jnp.concatenate(lines, axis=0) * f_ref[...]
    o_ref[...] = jnp.broadcast_to(y[None], o_ref.shape)


def target(at_ref, by, side):
    return 2 * around(at_ref, 0, by, 4) + around(at_ref, 1, side, 2)


def product_of(at_ref, ft_ref, w_ref, o_ref, by, side):
    feats = ft_ref[target(at_ref, by, side)]
    o_ref[...] = jnp.dot(feats, w_ref[...], preferred_element_type=F32)


def weight_body(e_ref, f_ref, a_ref, c_ref, fa_ref, k_ref, w_ref, m_ref):
    scale = (a_ref[...] / jnp.sum(e_ref[...], axis=0)) * f_ref[...]
    acc = [jnp.zeros((8, 128), F32)] * CB
    for b in range(RB):
        rows = slice(128 * b, 128 * b + 128)
        by = down(scale[b : b + 1])
        for t in range(CB):
            cols = slice(128 * t, 128 * t + 128)
            part = (k_ref[rows, cols] * by) * c_ref[t : t + 1, :]
            acc[t] = acc[t] + jnp.sum(part.reshape(16, 8, 128), axis=0)
            w_ref[rows, cols] = part.astype(BF16)
    m_ref[0:CB, :] = jnp.concatenate([jnp.sum(a, axis=0, keepdims=True) for a in acc], axis=0)
    m_ref[CB : CB + 8, :] = fa_ref[...]


def limits(at_ref, m, by):
    return m[0:CB, :] * m[pl.ds(CB + target(at_ref, by, 0), 1), :]


def inverse(q):
    return jnp.where(q > 0, 32768.0 / jnp.where(q > 0, q, 1.0), 0.0)


def chip_body(at_ref, ft_ref, w_ref, mine_ref, other_ref, o_ref, m_ref, i_ref):
    product_of(at_ref, ft_ref, w_ref, o_ref, 2, 0)
    m_ref[0:CB, :] = mine_ref[0:CB, :] + other_ref[0:CB, :]
    m_ref[CB : CB + 8, :] = jnp.maximum(mine_ref[CB : CB + 8, :], other_ref[CB : CB + 8, :])
    for k, by in enumerate((2, 1, 3)):
        i_ref[k] = inverse(limits(at_ref, m_ref, by))


def relay_body(at_ref, m0, m1, m3, i_ref, s_ref):
    for k, (m, by) in enumerate(((m1, 1), (m3, 3))):
        q = limits(at_ref, m, by)
        s_ref[k] = q * (1.0 / 32768.0)
        i_ref[k] = inverse(q + limits(at_ref, m0, by))


def share_body(at_ref, m0, m1, m2, m3, t_ref, i_ref, s_ref):
    total = (m0[0:CB, :] + m2[0:CB, :]) + (m1[0:CB, :] + m3[0:CB, :])
    t_ref[...] = total
    over = 1.0 / total
    i_ref[...] = over
    q1, q2, q3 = (limits(at_ref, m, 0) * (1.0 / 32768.0) for m in (m1, m2, m3))
    for k, q in enumerate((q1, q3, q1 + q2, q3 + q2)):
        s_ref[k] = q * over


def product_body(which, at_ref, ft_ref, w_ref, *o_refs):
    for k, o_ref in enumerate(o_refs):
        product_of(at_ref, ft_ref, w_ref, o_ref, *which[k])


def assigned(features, centroids, row_weight, centroid_share):
    y, core, z, x = (lax.axis_index(n) for n in ("y", "core", "z", "x"))
    at = jnp.stack([y, core, z, x]).astype(jnp.int32)
    a = row_weight.reshape(RB, 128)
    share = centroid_share.reshape(CB, 128)

    own = after(features.T, at)

    def ring(x, by):
        return step(x, "z", by)

    def scores(body, outs, ins, depth, aliases=None, more=()):
        return call(
            body,
            outs,
            ins,
            scratch=[pltpu.VMEM((ROWS, depth), BF16), pltpu.VMEM((COLS, depth), BF16), *more],
            mib=16,
            aliases=aliases,
        )

    parts = []
    for by in (1, -1, 2):
        parts.append(step(own, "x", by))
    strip_shape = [((128, ROWS), BF16)]
    (strip,) = call(own_body, strip_shape, [own], mib=4)
    (strip,) = call(join_body, strip_shape, [*parts, strip], mib=4, aliases={3: 0})
    state = [((ROWS, COLS), F32), ((8, 128, ROWS), BF16), ((8, 128), F32)]
    right = [strip, ring(strip, 1)]
    left = [strip, ring(strip, -1)]
    kernel, ft, fa = scores(score0_body, state, [at, strip, centroids], 128)
    for k in (1, 2):
        right.append(ring(right[k], 1))
        left.append(ring(left[k], -1))
    far = [ring(right[3][:64], 1), ring(left[3][64:], -1)]
    for k in (1, 2, 3):
        kernel, ft, fa = scores(
            functools.partial(score_body, k),
            state,
            [at, left[k], right[k], centroids, kernel, ft, fa],
            256,
            {4: 0, 5: 1, 6: 2},
        )
    kernel, ft, fa, peaks = scores(
        score4_body,
        [*state, ((32, 2 * RB, 128), F32)],
        [at, *far, centroids, kernel, ft, fa],
        128,
        {4: 0, 5: 1, 6: 2},
        [pltpu.VMEM((ROWS, 128), F32)] * 2,
    )
    lines = [pltpu.VMEM((ROWS, 128), F32)]
    got = everyone(peaks, CENT)
    sums, fold = call(
        first_column_body, [((8, CB, 128), F32), ((RB, 128), F32)], [got, peaks, a, kernel], mib=8
    )
    for it in range(ITERS):
        rows, *cscale = call(
            row_body,
            [((32, RB, 128), F32)] + [((CB, 128), F32)] * (it == ITERS - 1),
            [everyone(sums, DP), fold, share, kernel],
            scratch=lines,
            mib=8,
        )
        got = everyone(rows, CENT)
        if it < ITERS - 1:
            (sums,) = call(column_body, [((8, CB, 128), F32)], [got, fold, a, kernel], mib=8)
    weights, mass = call(
        weight_body,
        [((ROWS, COLS), BF16), ((CB + 8, 128), F32)],
        [got, fold, a, *cscale, fa, kernel],
        mib=8,
    )

    other = step(mass, "core", 1)

    def products(which, where):
        return call(
            functools.partial(product_body, which),
            [((128, COLS), F32)] * len(which),
            [where, ft, weights],
            mib=16,
        )

    def send(x, by):
        return step(x.astype(jnp.float16), "y", by)

    low, high = slice(0, 64), slice(64, 128)
    (give,) = products([(2, 1)], at)
    theirs = step(give, "core", 1)
    mine, chip, packs = call(
        chip_body,
        [((128, COLS), F32), ((CB + 8, 128), F32), ((3, CB, 128), F32)],
        [after(at, give), ft, weights, mass, other],
        mib=16,
    )
    packs = packs.reshape(3, 1, COLS)
    chips = {}
    for by, mass in ((1, chip), (3, chip), (2, None)):
        chips[by] = step(chips[1], "y", 1) if mass is None else step(mass, "y", by)
    up = ((mine[low] + theirs[low]) * packs[0]).astype(jnp.float16)
    down_ = ((mine[high] + theirs[high]) * packs[0]).astype(jnp.float16)
    first = (send(up, 1), send(down_, 3))
    gives = products([(1, 1), (3, 1)], after(at, up, down_))
    theirs = [step(g, "core", 1) for g in gives]
    mines = products([(1, 0), (3, 0)], after(at, *gives))
    up = ((mines[0][high] + theirs[0][high]) * packs[1]).astype(jnp.float16)
    down_ = ((mines[1][low] + theirs[1][low]) * packs[2]).astype(jnp.float16)
    second = (send(up, 1), send(down_, 3))
    repacks, unpacks = call(
        relay_body, [((2, CB, 128), F32)] * 2, [at, chip, chips[1], chips[3]], mib=4
    )
    repacks, unpacks = repacks.reshape(2, 1, COLS), unpacks.reshape(2, 1, COLS)
    give, mine0 = products([(0, 1), (0, 0)], at)
    theirs0 = step(give, "core", 1)
    total, over, shares = call(
        share_body,
        [((CB, 128), F32), ((CB, 128), F32), ((4, CB, 128), F32)],
        [at, chip, chips[1], chips[2], chips[3]],
        mib=4,
    )
    mines, theirs, *_ = lax.optimization_barrier((mines, theirs, up, down_))
    up = mines[0][low] + theirs[0][low] + first[0].astype(F32) * unpacks[0]
    down_ = mines[1][high] + theirs[1][high] + first[1].astype(F32) * unpacks[1]
    third = (send(up * repacks[0], 1), send(down_ * repacks[1], 3))

    over, shares = over.reshape(1, COLS), shares.reshape(4, 1, COLS)
    own_part = (mine0 + theirs0) * over
    top = own_part[low] + second[1].astype(F32) * shares[1] + third[0].astype(F32) * shares[2]
    bottom = own_part[high] + second[0].astype(F32) * shares[0] + third[1].astype(F32) * shares[3]
    return jnp.concatenate([top, bottom], axis=0), total.reshape(COLS)


def solution(mesh):
    split = Mesh(mesh.devices.reshape(4, 2, 8, 4), ("y", "core", "z", "x"))
    return jax.shard_map(
        assigned,
        mesh=split,
        in_specs=(P(DP, CENT), P(CENT, None), P(DP), P(CENT)),
        out_specs=(P(DP, CENT), P(CENT)),
        check_vma=False,
    )
```

```python
import functools

import jax
import jax.numpy as jnp
from jax import lax
from jax.experimental import pallas as pl
from jax.experimental.pallas import tpu as pltpu
from jax.sharding import Mesh
from jax.sharding import PartitionSpec as P

ITERS = 3
ROWS = 1024
COLS = 2048
RB, CB = ROWS // 128, COLS // 128
CENT = ("z", "x")
DP = ("y", "core")
F32, BF16 = jnp.float32, jnp.bfloat16
VM = pl.BlockSpec(memory_space=pltpu.VMEM)
SM = pl.BlockSpec(memory_space=pltpu.SMEM)


def call(body, outs, ins, scratch=(), mib=24, aliases=None):
    return pl.pallas_call(
        body,
        out_shape=[jax.ShapeDtypeStruct(s, d) for s, d in outs],
        in_specs=[SM if a.dtype == jnp.int32 else VM for a in ins],
        out_specs=[VM] * len(outs),
        scratch_shapes=list(scratch),
        input_output_aliases=aliases or {},
        compiler_params=pltpu.CompilerParams(vmem_limit_bytes=mib << 20),
    )(*ins)


def step(x, axis, by):
    n = lax.axis_size(axis)
    return lax.ppermute(x, axis, [(i, (i + by) % n) for i in range(n)])


def step_apart(x):
    ends = [(c, i, (i + 1 - 2 * c) % 4) for c in (0, 1) for i in range(4)]
    return lax.ppermute(x, DP, [(2 * i + c, 2 * j + c) for c, i, j in ends])


def everyone(x, axis):
    return lax.all_to_all(x, axis, 0, 0, tiled=True)


def after(x, *others):
    return lax.optimization_barrier((x, *others))[0]


def down(row):
    return jnp.broadcast_to(row, (128, 128)).T


def around(at_ref, k, by, n):
    return lax.rem(at_ref[k] + (n + by), n)


def own_body(a_ref, o_ref):
    o_ref[0:32, :] = a_ref[...]


def join_body(b_ref, c_ref, d_ref, in_ref, o_ref):
    for k, ref in enumerate((b_ref, c_ref, d_ref)):
        o_ref[32 * k + 32 : 32 * k + 64, :] = ref[...]


def collect(at_ref, pieces, c_ref, ft_ref, fa_ref, fs_ref, cs_ref):
    for k, (by, parts) in enumerate(pieces):
        at = around(at_ref, 2, by, 8)
        for (ref, row), off in zip(parts, (0, -1, 1, 2)):
            place = pl.multiple_of(32 * around(at_ref, 3, off, 4), 32)
            ft_ref[at, pl.ds(place, 32), :] = ref[row : row + 32, :]
        piece = ft_ref[at]
        top = jnp.max(jnp.abs(piece), axis=0, keepdims=True).astype(F32)
        fa_ref[pl.ds(at, 1), :] = jnp.broadcast_to(jnp.max(top, axis=1, keepdims=True), (1, 128))
        fs_ref[:, 128 * k : 128 * k + 128] = piece.T
        cs_ref[:, 128 * k : 128 * k + 128] = c_ref[:, pl.ds(pl.multiple_of(at * 128, 128), 128)]


def product(f, c):
    return lax.dot_general(f, c, (((1,), (1,)), ((), ())), preferred_element_type=F32)


def whole(ref):
    return [(ref, 32 * k) for k in range(4)]


def accumulate(kin, k_ref, fs, cs):
    def block(b, carry):
        rows = pl.ds(pl.multiple_of(256 * b, 256), 256)
        s = product(fs[rows, :], cs[...])
        k_ref[rows, :] = s if kin is None else kin[rows, :] + s
        return carry

    lax.fori_loop(0, 4, block, 0)


def score0_body(at_ref, s_ref, c_ref, k_ref, ft_ref, fa_ref, fs, cs):
    collect(at_ref, [(0, whole(s_ref))], c_ref, ft_ref, fa_ref, fs, cs)
    accumulate(None, k_ref, fs, cs)


def score_body(by, at_ref, l, r, c_ref, kin, ftin, fain, k_ref, ft_ref, fa_ref, fs, cs):
    collect(at_ref, [(by, whole(l)), (-by, whole(r))], c_ref, ft_ref, fa_ref, fs, cs)
    accumulate(kin, k_ref, fs, cs)


def score4_body(at_ref, h0, h1, c_ref, kin, ftin, fain, k_ref, ft_ref, fa_ref, p_ref, fs, cs, tops, sums):
    far = (4, [(h0, 0), (h0, 32), (h1, 0), (h1, 32)])
    collect(at_ref, [far], c_ref, ft_ref, fa_ref, fs, cs)

    def scored(b):
        rows = pl.ds(pl.multiple_of(128 * b, 128), 128)
        s = kin[rows, :] + product(fs[rows, :], cs[...])
        k_ref[rows, :] = s
        tops[rows, :] = jnp.broadcast_to(jnp.max(s, axis=1, keepdims=True), (128, 128))

    def raised(b):
        rows = pl.ds(pl.multiple_of(128 * b, 128), 128)
        top, acc = tops[rows, :], jnp.zeros((128, 128), F32)
        for t in range(CB):
            cols = slice(128 * t, 128 * t + 128)
            e = jnp.exp(k_ref[rows, cols] - top)
            k_ref[rows, cols] = e
            acc = acc + e
        sums[rows, :] = acc

    def block(b, carry):
        raised(b)
        scored(b + 1)
        return carry

    scored(0)
    lax.fori_loop(0, RB - 1, block, 0)
    raised(RB - 1)
    lines = [tops[128 * b : 128 * b + 128, :].T[0:1] for b in range(RB)]
    lines += [jnp.sum(sums[128 * b : 128 * b + 128, :].T, axis=0, keepdims=True) for b in range(RB)]
    p_ref[...] = jnp.broadcast_to(jnp.concatenate(lines, axis=0)[None], p_ref.shape)


def columns(k_ref, scale, o_ref):
    acc = [jnp.zeros((8, 128), F32)] * CB
    for b in range(RB):
        rows = slice(128 * b, 128 * b + 128)
        by = down(scale[b : b + 1])
        for t in range(CB):
            part = k_ref[rows, 128 * t : 128 * t + 128] * by
            acc[t] = acc[t] + jnp.sum(part.reshape(16, 8, 128), axis=0)
    z = jnp.concatenate([jnp.sum(a, axis=0, keepdims=True) for a in acc], axis=0)
    o_ref[...] = jnp.broadcast_to(z[None], o_ref.shape)


def first_column_body(e_ref, mine_ref, a_ref, k_ref, o_ref, f_ref):
    peaks = e_ref[:, 0:RB, :]
    top = jnp.max(peaks, axis=0)
    total = jnp.sum(e_ref[:, RB : 2 * RB, :] * jnp.exp(peaks - top[None]), axis=0)
    fold = jnp.exp(mine_ref[0, 0:RB, :] - top)
    f_ref[...] = fold
    columns(k_ref, (a_ref[...] / total) * fold, o_ref)


def column_body(e_ref, f_ref, a_ref, k_ref, o_ref):
    scale = a_ref[...] / jnp.sum(e_ref[...], axis=0)
    columns(k_ref, scale * f_ref[...], o_ref)


def row_body(e_ref, f_ref, b_ref, k_ref, o_ref, *refs):
    scale = b_ref[...] / jnp.sum(e_ref[...], axis=0)
    acc_ref = refs[-1]
    if len(refs) > 1:
        refs[0][...] = scale

    def block(b, carry):
        rows = pl.ds(pl.multiple_of(128 * b, 128), 128)
        acc = jnp.zeros((128, 128), F32)
        for t in range(CB):
            acc = acc + k_ref[rows, 128 * t : 128 * t + 128] * scale[t : t + 1]
        acc_ref[rows, :] = acc
        return carry

    lax.fori_loop(0, RB, block, 0)
    lines = [
        jnp.sum(acc_ref[128 * b : 128 * b + 128, :].T, axis=0, keepdims=True) for b in range(RB)
    ]
    y = jnp.concatenate(lines, axis=0) * f_ref[...]
    o_ref[...] = jnp.broadcast_to(y[None], o_ref.shape)


def target(at_ref, by, side):
    return 2 * around(at_ref, 0, by, 4) + around(at_ref, 1, side, 2)


def product_of(at_ref, ft_ref, w_ref, o_ref, by, side):
    feats = ft_ref[target(at_ref, by, side)]
    o_ref[...] = jnp.dot(feats, w_ref[...], preferred_element_type=F32)


def weight_body(e_ref, f_ref, a_ref, c_ref, fa_ref, k_ref, w_ref, m_ref):
    scale = (a_ref[...] / jnp.sum(e_ref[...], axis=0)) * f_ref[...]
    acc = [jnp.zeros((8, 128), F32)] * CB
    for b in range(RB):
        rows = slice(128 * b, 128 * b + 128)
        by = down(scale[b : b + 1])
        for t in range(CB):
            cols = slice(128 * t, 128 * t + 128)
            part = (k_ref[rows, cols] * by) * c_ref[t : t + 1, :]
            acc[t] = acc[t] + jnp.sum(part.reshape(16, 8, 128), axis=0)
            w_ref[rows, cols] = part.astype(BF16)
    m_ref[0:CB, :] = jnp.concatenate([jnp.sum(a, axis=0, keepdims=True) for a in acc], axis=0)
    m_ref[CB : CB + 8, :] = fa_ref[...]


def limits(at_ref, m, by):
    return m[0:CB, :] * m[pl.ds(CB + target(at_ref, by, 0), 1), :]


def inverse(q):
    return jnp.where(q > 0, 32768.0 / jnp.where(q > 0, q, 1.0), 0.0)


def chip_body(at_ref, ft_ref, w_ref, mine_ref, other_ref, o_ref, m_ref, i_ref):
    product_of(at_ref, ft_ref, w_ref, o_ref, 2, 0)
    m_ref[0:CB, :] = mine_ref[0:CB, :] + other_ref[0:CB, :]
    m_ref[CB : CB + 8, :] = jnp.maximum(mine_ref[CB : CB + 8, :], other_ref[CB : CB + 8, :])
    for k, by in enumerate((2, 1, 3)):
        i_ref[k] = inverse(limits(at_ref, m_ref, by))


def sides(at_ref, near, other):
    first = at_ref[1] == 0
    return jnp.where(first, near[...], other[...]), jnp.where(first, other[...], near[...])


def limits_of(at_ref, m, ref, by):
    ref[...] = m
    return limits(at_ref, ref, by)


def relay_body(at_ref, m0, near, other, i_ref, s_ref, tmp):
    for k, (m, by) in enumerate(zip(sides(at_ref, near, other), (1, 3))):
        q = limits_of(at_ref, m, tmp, by)
        s_ref[k] = q * (1.0 / 32768.0)
        i_ref[k] = inverse(q + limits(at_ref, m0, by))


def share_body(at_ref, m0, near, m2, other, t_ref, i_ref, s_ref, tmp):
    m1, m3 = sides(at_ref, near, other)
    total = (m0[0:CB, :] + m2[0:CB, :]) + (m1[0:CB, :] + m3[0:CB, :])
    t_ref[...] = total
    over = 1.0 / total
    i_ref[...] = over
    q1, q3 = (limits_of(at_ref, m, tmp, 0) * (1.0 / 32768.0) for m in (m1, m3))
    q2 = limits(at_ref, m2, 0) * (1.0 / 32768.0)
    for k, q in enumerate((q1, q3, q1 + q2, q3 + q2)):
        s_ref[k] = q * over


def product_body(which, at_ref, ft_ref, w_ref, *o_refs):
    for k, o_ref in enumerate(o_refs):
        product_of(at_ref, ft_ref, w_ref, o_ref, *which[k])


def assigned(features, centroids, row_weight, centroid_share):
    y, core, z, x = (lax.axis_index(n) for n in ("y", "core", "z", "x"))
    at = jnp.stack([y, core, z, x]).astype(jnp.int32)
    a = row_weight.reshape(RB, 128)
    share = centroid_share.reshape(CB, 128)

    own = after(features.T, at)

    def ring(x, by):
        return step(x, "z", by)

    def scores(body, outs, ins, depth, aliases=None, more=()):
        return call(
            body,
            outs,
            ins,
            scratch=[pltpu.VMEM((ROWS, depth), BF16), pltpu.VMEM((COLS, depth), BF16), *more],
            mib=16,
            aliases=aliases,
        )

    parts = []
    for by in (1, -1, 2):
        parts.append(step(own, "x", by))
    strip_shape = [((128, ROWS), BF16)]
    (strip,) = call(own_body, strip_shape, [own], mib=4)
    (strip,) = call(join_body, strip_shape, [*parts, strip], mib=4, aliases={3: 0})
    state = [((ROWS, COLS), F32), ((8, 128, ROWS), BF16), ((8, 128), F32)]
    right = [strip, ring(strip, 1)]
    left = [strip, ring(strip, -1)]
    kernel, ft, fa = scores(score0_body, state, [at, strip, centroids], 128)
    for k in (1, 2):
        right.append(ring(right[k], 1))
        left.append(ring(left[k], -1))
    far = [ring(right[3][:64], 1), ring(left[3][64:], -1)]
    for k in (1, 2, 3):
        kernel, ft, fa = scores(
            functools.partial(score_body, k),
            state,
            [at, left[k], right[k], centroids, kernel, ft, fa],
            256,
            {4: 0, 5: 1, 6: 2},
        )
    kernel, ft, fa, peaks = scores(
        score4_body,
        [*state, ((32, 2 * RB, 128), F32)],
        [at, *far, centroids, kernel, ft, fa],
        128,
        {4: 0, 5: 1, 6: 2},
        [pltpu.VMEM((ROWS, 128), F32)] * 2,
    )
    lines = [pltpu.VMEM((ROWS, 128), F32)]
    got = everyone(peaks, CENT)
    sums, fold = call(
        first_column_body, [((8, CB, 128), F32), ((RB, 128), F32)], [got, peaks, a, kernel], mib=8
    )
    for it in range(ITERS):
        rows, *cscale = call(
            row_body,
            [((32, RB, 128), F32)] + [((CB, 128), F32)] * (it == ITERS - 1),
            [everyone(sums, DP), fold, share, kernel],
            scratch=lines,
            mib=8,
        )
        got = everyone(rows, CENT)
        if it < ITERS - 1:
            (sums,) = call(column_body, [((8, CB, 128), F32)], [got, fold, a, kernel], mib=8)
    weights, mass = call(
        weight_body,
        [((ROWS, COLS), BF16), ((CB + 8, 128), F32)],
        [got, fold, a, *cscale, fa, kernel],
        mib=8,
    )

    other = step(mass, "core", 1)

    def products(which, where):
        return call(
            functools.partial(product_body, which),
            [((128, COLS), F32)] * len(which),
            [where, ft, weights],
            mib=16,
        )

    def send(x, by):
        return step(x.astype(jnp.float16), "y", by)

    low, high = slice(0, 64), slice(64, 128)
    (give,) = products([(2, 1)], at)
    theirs = step(give, "core", 1)
    mine, chip, packs = call(
        chip_body,
        [((128, COLS), F32), ((CB + 8, 128), F32), ((3, CB, 128), F32)],
        [after(at, give), ft, weights, mass, other],
        mib=16,
    )
    packs = packs.reshape(3, 1, COLS)
    near = step_apart(chip)
    other_near = step(near, "core", 1)
    far_mass = step_apart(near)
    up = ((mine[low] + theirs[low]) * packs[0]).astype(jnp.float16)
    down_ = ((mine[high] + theirs[high]) * packs[0]).astype(jnp.float16)
    first = (send(up, 1), send(down_, 3))
    gives = products([(1, 1), (3, 1)], after(at, up, down_))
    theirs = [step(g, "core", 1) for g in gives]
    mines = products([(1, 0), (3, 0)], after(at, *gives))
    up = ((mines[0][high] + theirs[0][high]) * packs[1]).astype(jnp.float16)
    down_ = ((mines[1][low] + theirs[1][low]) * packs[2]).astype(jnp.float16)
    second = (send(up, 1), send(down_, 3))
    repacks, unpacks = call(
        relay_body,
        [((2, CB, 128), F32)] * 2,
        [at, chip, near, other_near],
        scratch=[pltpu.VMEM((CB + 8, 128), F32)],
        mib=4,
    )
    repacks, unpacks = repacks.reshape(2, 1, COLS), unpacks.reshape(2, 1, COLS)
    give, mine0 = products([(0, 1), (0, 0)], at)
    theirs0 = step(give, "core", 1)
    total, over, shares = call(
        share_body,
        [((CB, 128), F32), ((CB, 128), F32), ((4, CB, 128), F32)],
        [at, chip, near, far_mass, other_near],
        scratch=[pltpu.VMEM((CB + 8, 128), F32)],
        mib=4,
    )
    mines, theirs, *_ = lax.optimization_barrier((mines, theirs, up, down_))
    up = mines[0][low] + theirs[0][low] + first[0].astype(F32) * unpacks[0]
    down_ = mines[1][high] + theirs[1][high] + first[1].astype(F32) * unpacks[1]
    third = (send(up * repacks[0], 1), send(down_ * repacks[1], 3))

    over, shares = over.reshape(1, COLS), shares.reshape(4, 1, COLS)
    own_part = (mine0 + theirs0) * over
    top = own_part[low] + second[1].astype(F32) * shares[1] + third[0].astype(F32) * shares[2]
    bottom = own_part[high] + second[0].astype(F32) * shares[0] + third[1].astype(F32) * shares[3]
    return jnp.concatenate([top, bottom], axis=0), total.reshape(COLS)


def solution(mesh):
    split = Mesh(mesh.devices.reshape(4, 2, 8, 4), ("y", "core", "z", "x"))
    return jax.shard_map(
        assigned,
        mesh=split,
        in_specs=(P(DP, CENT), P(CENT, None), P(DP), P(CENT)),
        out_specs=(P(DP, CENT), P(CENT)),
        check_vma=False,
    )
```

```python
import functools

import jax
import jax.numpy as jnp
from jax import lax
from jax.experimental import pallas as pl
from jax.experimental.pallas import tpu as pltpu
from jax.sharding import Mesh
from jax.sharding import PartitionSpec as P

ITERS = 3
ROWS = 1024
COLS = 2048
RB, CB = ROWS // 128, COLS // 128
CENT = ("z", "x")
DP = ("y", "core")
F32, BF16 = jnp.float32, jnp.bfloat16
VM = pl.BlockSpec(memory_space=pltpu.VMEM)
SM = pl.BlockSpec(memory_space=pltpu.SMEM)


def call(body, outs, ins, scratch=(), mib=24, aliases=None):
    return pl.pallas_call(
        body,
        out_shape=[jax.ShapeDtypeStruct(s, d) for s, d in outs],
        in_specs=[SM if a.dtype == jnp.int32 else VM for a in ins],
        out_specs=[VM] * len(outs),
        scratch_shapes=list(scratch),
        input_output_aliases=aliases or {},
        compiler_params=pltpu.CompilerParams(vmem_limit_bytes=mib << 20),
    )(*ins)


def step(x, axis, by):
    n = lax.axis_size(axis)
    return lax.ppermute(x, axis, [(i, (i + by) % n) for i in range(n)])


def step_apart(x):
    ends = [(c, i, (i + 1 - 2 * c) % 4) for c in (0, 1) for i in range(4)]
    return lax.ppermute(x, DP, [(2 * i + c, 2 * j + c) for c, i, j in ends])


def everyone(x, axis):
    return lax.all_to_all(x, axis, 0, 0, tiled=True)


def after(x, *others):
    return lax.optimization_barrier((x, *others))[0]


def down(row):
    return jnp.broadcast_to(row, (128, 128)).T


def around(at_ref, k, by, n):
    return lax.rem(at_ref[k] + (n + by), n)


def own_body(a_ref, o_ref):
    o_ref[0:32, :] = a_ref[...]


def join_body(b_ref, c_ref, d_ref, in_ref, o_ref):
    for k, ref in enumerate((b_ref, c_ref, d_ref)):
        o_ref[32 * k + 32 : 32 * k + 64, :] = ref[...]


def collect(at_ref, pieces, c_ref, ft_ref, fa_ref, fs_ref, cs_ref):
    for k, (by, parts) in enumerate(pieces):
        at = around(at_ref, 2, by, 8)
        for (ref, row), off in zip(parts, (0, -1, 1, 2)):
            place = pl.multiple_of(32 * around(at_ref, 3, off, 4), 32)
            ft_ref[at, pl.ds(place, 32), :] = ref[row : row + 32, :]
        piece = ft_ref[at]
        top = jnp.max(jnp.abs(piece), axis=0, keepdims=True).astype(F32)
        fa_ref[pl.ds(at, 1), :] = jnp.broadcast_to(jnp.max(top, axis=1, keepdims=True), (1, 128))
        fs_ref[:, 128 * k : 128 * k + 128] = piece.T
        cs_ref[:, 128 * k : 128 * k + 128] = c_ref[:, pl.ds(pl.multiple_of(at * 128, 128), 128)]


def product(f, c):
    return lax.dot_general(f, c, (((1,), (1,)), ((), ())), preferred_element_type=F32)


def whole(ref):
    return [(ref, 32 * k) for k in range(4)]


def accumulate(kin, k_ref, fs, cs):
    def block(b, carry):
        rows = pl.ds(pl.multiple_of(256 * b, 256), 256)
        s = product(fs[rows, :], cs[...])
        k_ref[rows, :] = s if kin is None else kin[rows, :] + s
        return carry

    lax.fori_loop(0, 4, block, 0)


def score0_body(at_ref, s_ref, c_ref, k_ref, ft_ref, fa_ref, fs, cs):
    collect(at_ref, [(0, whole(s_ref))], c_ref, ft_ref, fa_ref, fs, cs)
    accumulate(None, k_ref, fs, cs)


def score_body(by, at_ref, l, r, c_ref, kin, ftin, fain, k_ref, ft_ref, fa_ref, fs, cs):
    collect(at_ref, [(by, whole(l)), (-by, whole(r))], c_ref, ft_ref, fa_ref, fs, cs)
    accumulate(kin, k_ref, fs, cs)


def score4_body(at_ref, h0, h1, c_ref, kin, ftin, fain, k_ref, ft_ref, fa_ref, p_ref, fs, cs, tops, sums):
    far = (4, [(h0, 0), (h0, 32), (h1, 0), (h1, 32)])
    collect(at_ref, [far], c_ref, ft_ref, fa_ref, fs, cs)

    def scored(b):
        rows = pl.ds(pl.multiple_of(128 * b, 128), 128)
        s = kin[rows, :] + product(fs[rows, :], cs[...])
        k_ref[rows, :] = s
        tops[rows, :] = jnp.broadcast_to(jnp.max(s, axis=1, keepdims=True), (128, 128))

    def raised(b):
        rows = pl.ds(pl.multiple_of(128 * b, 128), 128)
        top, acc = tops[rows, :], jnp.zeros((128, 128), F32)
        for t in range(CB):
            cols = slice(128 * t, 128 * t + 128)
            e = jnp.exp(k_ref[rows, cols] - top)
            k_ref[rows, cols] = e
            acc = acc + e
        sums[rows, :] = acc

    def block(b, carry):
        raised(b)
        scored(b + 1)
        return carry

    scored(0)
    lax.fori_loop(0, RB - 1, block, 0)
    raised(RB - 1)
    lines = [tops[128 * b : 128 * b + 128, :].T[0:1] for b in range(RB)]
    lines += [jnp.sum(sums[128 * b : 128 * b + 128, :].T, axis=0, keepdims=True) for b in range(RB)]
    p_ref[...] = jnp.broadcast_to(jnp.concatenate(lines, axis=0)[None], p_ref.shape)


def columns(k_ref, scale, o_ref):
    acc = [jnp.zeros((8, 128), F32)] * CB
    for b in range(RB):
        rows = slice(128 * b, 128 * b + 128)
        by = down(scale[b : b + 1])
        for t in range(CB):
            part = k_ref[rows, 128 * t : 128 * t + 128] * by
            acc[t] = acc[t] + jnp.sum(part.reshape(16, 8, 128), axis=0)
    z = jnp.concatenate([jnp.sum(a, axis=0, keepdims=True) for a in acc], axis=0)
    o_ref[...] = jnp.broadcast_to(z[None], o_ref.shape)


def first_column_body(e_ref, mine_ref, a_ref, k_ref, o_ref, f_ref):
    peaks = e_ref[:, 0:RB, :]
    top = jnp.max(peaks, axis=0)
    total = jnp.sum(e_ref[:, RB : 2 * RB, :] * jnp.exp(peaks - top[None]), axis=0)
    fold = jnp.exp(mine_ref[0, 0:RB, :] - top)
    f_ref[...] = fold
    columns(k_ref, (a_ref[...] / total) * fold, o_ref)


def column_body(e_ref, f_ref, a_ref, k_ref, o_ref):
    scale = a_ref[...] / jnp.sum(e_ref[...], axis=0)
    columns(k_ref, scale * f_ref[...], o_ref)


def row_body(e_ref, f_ref, b_ref, k_ref, o_ref, *refs):
    scale = b_ref[...] / jnp.sum(e_ref[...], axis=0)
    acc_ref = refs[-1]
    if len(refs) > 1:
        refs[0][...] = scale
    small = scale * 2.0**-12

    def block(b, carry):
        rows = pl.ds(pl.multiple_of(128 * b, 128), 128)
        acc = jnp.zeros((128, 128), F32)
        for t in range(CB):
            acc = acc + k_ref[rows, 128 * t : 128 * t + 128] * small[t : t + 1]
        acc_ref[rows, :] = acc
        return carry

    lax.fori_loop(0, RB, block, 0)
    lines = [
        jnp.sum(acc_ref[128 * b : 128 * b + 128, :].T, axis=0, keepdims=True) for b in range(RB)
    ]
    y = jnp.concatenate(lines, axis=0) * (f_ref[...] * 2.0**12)
    o_ref[...] = jnp.broadcast_to(y[None], o_ref.shape)


def target(at_ref, by, side):
    return 2 * around(at_ref, 0, by, 4) + around(at_ref, 1, side, 2)


def product_of(at_ref, ft_ref, w_ref, o_ref, by, side):
    feats = ft_ref[target(at_ref, by, side)]
    o_ref[...] = jnp.dot(feats, w_ref[...], preferred_element_type=F32)


def weight_body(e_ref, f_ref, a_ref, c_ref, fa_ref, k_ref, w_ref, m_ref):
    scale = (a_ref[...] / jnp.sum(e_ref[...], axis=0)) * f_ref[...]
    acc = [jnp.zeros((8, 128), F32)] * CB
    for b in range(RB):
        rows = slice(128 * b, 128 * b + 128)
        by = down(scale[b : b + 1])
        for t in range(CB):
            cols = slice(128 * t, 128 * t + 128)
            part = (k_ref[rows, cols] * by) * c_ref[t : t + 1, :]
            acc[t] = acc[t] + jnp.sum(part.reshape(16, 8, 128), axis=0)
            w_ref[rows, cols] = part.astype(BF16)
    m_ref[0:CB, :] = jnp.concatenate([jnp.sum(a, axis=0, keepdims=True) for a in acc], axis=0)
    m_ref[CB : CB + 8, :] = fa_ref[...]


def limits(at_ref, m, by):
    return jnp.maximum(m[0:CB, :] * m[pl.ds(CB + target(at_ref, by, 0), 1), :], 2.0**-100)


def inverse(q):
    return 32768.0 / q


def chip_body(at_ref, ft_ref, w_ref, mine_ref, other_ref, o_ref, m_ref, i_ref):
    product_of(at_ref, ft_ref, w_ref, o_ref, 2, 0)
    m_ref[0:CB, :] = mine_ref[0:CB, :] + other_ref[0:CB, :]
    m_ref[CB : CB + 8, :] = jnp.maximum(mine_ref[CB : CB + 8, :], other_ref[CB : CB + 8, :])
    for k, by in enumerate((2, 1, 3)):
        i_ref[k] = inverse(limits(at_ref, m_ref, by))


def sides(at_ref, near, other):
    first = at_ref[1] == 0
    return jnp.where(first, near[...], other[...]), jnp.where(first, other[...], near[...])


def limits_of(at_ref, m, ref, by):
    ref[...] = m
    return limits(at_ref, ref, by)


def relay_body(at_ref, m0, near, other, i_ref, s_ref, tmp):
    for k, (m, by) in enumerate(zip(sides(at_ref, near, other), (1, 3))):
        q = limits_of(at_ref, m, tmp, by)
        s_ref[k] = q * (1.0 / 32768.0)
        i_ref[k] = inverse(q + limits(at_ref, m0, by))


def share_body(at_ref, m0, near, m2, other, t_ref, i_ref, s_ref, tmp):
    m1, m3 = sides(at_ref, near, other)
    total = (m0[0:CB, :] + m2[0:CB, :]) + (m1[0:CB, :] + m3[0:CB, :])
    t_ref[...] = total
    over = 1.0 / total
    i_ref[...] = over
    q1, q3 = (limits_of(at_ref, m, tmp, 0) * (1.0 / 32768.0) for m in (m1, m3))
    q2 = limits(at_ref, m2, 0) * (1.0 / 32768.0)
    for k, q in enumerate((q1, q3, q1 + q2, q3 + q2)):
        s_ref[k] = q * over


def product_body(which, at_ref, ft_ref, w_ref, *o_refs):
    for k, o_ref in enumerate(o_refs):
        product_of(at_ref, ft_ref, w_ref, o_ref, *which[k])


def assigned(features, centroids, row_weight, centroid_share):
    y, core, z, x = (lax.axis_index(n) for n in ("y", "core", "z", "x"))
    at = jnp.stack([y, core, z, x]).astype(jnp.int32)
    a = row_weight.reshape(RB, 128)
    share = centroid_share.reshape(CB, 128)

    own = after(features.T, at)

    def ring(x, by):
        return step(x, "z", by)

    def scores(body, outs, ins, depth, aliases=None, more=()):
        return call(
            body,
            outs,
            ins,
            scratch=[pltpu.VMEM((ROWS, depth), BF16), pltpu.VMEM((COLS, depth), BF16), *more],
            mib=16,
            aliases=aliases,
        )

    parts = []
    for by in (1, -1, 2):
        parts.append(step(own, "x", by))
    strip_shape = [((128, ROWS), BF16)]
    (strip,) = call(own_body, strip_shape, [own], mib=4)
    (strip,) = call(join_body, strip_shape, [*parts, strip], mib=4, aliases={3: 0})
    state = [((ROWS, COLS), F32), ((8, 128, ROWS), BF16), ((8, 128), F32)]
    right = [strip, ring(strip, 1)]
    left = [strip, ring(strip, -1)]
    kernel, ft, fa = scores(score0_body, state, [at, strip, centroids], 128)
    for k in (1, 2):
        right.append(ring(right[k], 1))
        left.append(ring(left[k], -1))
    far = [ring(right[3][:64], 1), ring(left[3][64:], -1)]
    for k in (1, 2, 3):
        kernel, ft, fa = scores(
            functools.partial(score_body, k),
            state,
            [at, left[k], right[k], centroids, kernel, ft, fa],
            256,
            {4: 0, 5: 1, 6: 2},
        )
    kernel, ft, fa, peaks = scores(
        score4_body,
        [*state, ((32, 2 * RB, 128), F32)],
        [at, *far, centroids, kernel, ft, fa],
        128,
        {4: 0, 5: 1, 6: 2},
        [pltpu.VMEM((ROWS, 128), F32)] * 2,
    )
    lines = [pltpu.VMEM((ROWS, 128), F32)]
    got = everyone(peaks, CENT)
    sums, fold = call(
        first_column_body, [((8, CB, 128), F32), ((RB, 128), F32)], [got, peaks, a, kernel], mib=8
    )
    for it in range(ITERS):
        rows, *cscale = call(
            row_body,
            [((32, RB, 128), F32)] + [((CB, 128), F32)] * (it == ITERS - 1),
            [everyone(sums, DP), fold, share, kernel],
            scratch=lines,
            mib=8,
        )
        got = everyone(rows, CENT)
        if it < ITERS - 1:
            (sums,) = call(column_body, [((8, CB, 128), F32)], [got, fold, a, kernel], mib=8)
    weights, mass = call(
        weight_body,
        [((ROWS, COLS), BF16), ((CB + 8, 128), F32)],
        [got, fold, a, *cscale, fa, kernel],
        mib=8,
    )

    other = step(mass, "core", 1)

    def products(which, where):
        return call(
            functools.partial(product_body, which),
            [((128, COLS), F32)] * len(which),
            [where, ft, weights],
            mib=16,
        )

    def send(x, by):
        return step(x.astype(jnp.float16), "y", by)

    low, high = slice(0, 64), slice(64, 128)
    (give,) = products([(2, 1)], at)
    theirs = step(give, "core", 1)
    mine, chip, packs = call(
        chip_body,
        [((128, COLS), F32), ((CB + 8, 128), F32), ((3, CB, 128), F32)],
        [after(at, give), ft, weights, mass, other],
        mib=16,
    )
    packs = packs.reshape(3, 1, COLS)
    near = step_apart(chip)
    other_near = step(near, "core", 1)
    far_mass = step_apart(near)
    up = ((mine[low] + theirs[low]) * packs[0]).astype(jnp.float16)
    down_ = ((mine[high] + theirs[high]) * packs[0]).astype(jnp.float16)
    first = (send(up, 1), send(down_, 3))
    gives = products([(1, 1), (3, 1)], after(at, up, down_))
    theirs = [step(g, "core", 1) for g in gives]
    mines = products([(1, 0), (3, 0)], after(at, *gives))
    up = ((mines[0][high] + theirs[0][high]) * packs[1]).astype(jnp.float16)
    down_ = ((mines[1][low] + theirs[1][low]) * packs[2]).astype(jnp.float16)
    second = (send(up, 1), send(down_, 3))
    repacks, unpacks = call(
        relay_body,
        [((2, CB, 128), F32)] * 2,
        [at, chip, near, other_near],
        scratch=[pltpu.VMEM((CB + 8, 128), F32)],
        mib=4,
    )
    repacks, unpacks = repacks.reshape(2, 1, COLS), unpacks.reshape(2, 1, COLS)
    give, mine0 = products([(0, 1), (0, 0)], at)
    theirs0 = step(give, "core", 1)
    total, over, shares = call(
        share_body,
        [((CB, 128), F32), ((CB, 128), F32), ((4, CB, 128), F32)],
        [at, chip, near, far_mass, other_near],
        scratch=[pltpu.VMEM((CB + 8, 128), F32)],
        mib=4,
    )
    mines, theirs, *_ = lax.optimization_barrier((mines, theirs, up, down_))
    up = mines[0][low] + theirs[0][low] + first[0].astype(F32) * unpacks[0]
    down_ = mines[1][high] + theirs[1][high] + first[1].astype(F32) * unpacks[1]
    third = (send(up * repacks[0], 1), send(down_ * repacks[1], 3))

    over, shares = over.reshape(1, COLS), shares.reshape(4, 1, COLS)
    own_part = (mine0 + theirs0) * over
    top = own_part[low] + second[1].astype(F32) * shares[1] + third[0].astype(F32) * shares[2]
    bottom = own_part[high] + second[0].astype(F32) * shares[0] + third[1].astype(F32) * shares[3]
    return jnp.concatenate([top, bottom], axis=0), total.reshape(COLS)


def solution(mesh):
    split = Mesh(mesh.devices.reshape(4, 2, 8, 4), ("y", "core", "z", "x"))
    return jax.shard_map(
        assigned,
        mesh=split,
        in_specs=(P(DP, CENT), P(CENT, None), P(DP), P(CENT)),
        out_specs=(P(DP, CENT), P(CENT)),
        check_vma=False,
    )
```

```python
import functools

import jax
import jax.numpy as jnp
from jax import lax
from jax.experimental import pallas as pl
from jax.experimental.pallas import tpu as pltpu
from jax.sharding import Mesh
from jax.sharding import PartitionSpec as P

ITERS = 3
ROWS = 1024
COLS = 2048
RB, CB = ROWS // 128, COLS // 128
CENT = ("z", "x")
DP = ("y", "core")
F32, BF16 = jnp.float32, jnp.bfloat16
VM = pl.BlockSpec(memory_space=pltpu.VMEM)
SM = pl.BlockSpec(memory_space=pltpu.SMEM)


def call(body, outs, ins, scratch=(), mib=24, aliases=None):
    return pl.pallas_call(
        body,
        out_shape=[jax.ShapeDtypeStruct(s, d) for s, d in outs],
        in_specs=[SM if a.dtype == jnp.int32 else VM for a in ins],
        out_specs=[VM] * len(outs),
        scratch_shapes=list(scratch),
        input_output_aliases=aliases or {},
        compiler_params=pltpu.CompilerParams(vmem_limit_bytes=mib << 20),
    )(*ins)


def step(x, axis, by):
    n = lax.axis_size(axis)
    return lax.ppermute(x, axis, [(i, (i + by) % n) for i in range(n)])


def step_apart(x):
    ends = [(c, i, (i + 1 - 2 * c) % 4) for c in (0, 1) for i in range(4)]
    return lax.ppermute(x, DP, [(2 * i + c, 2 * j + c) for c, i, j in ends])


def everyone(x, axis):
    return lax.all_to_all(x, axis, 0, 0, tiled=True)


def after(x, *others):
    return lax.optimization_barrier((x, *others))[0]


def down(row):
    return jnp.broadcast_to(row, (128, 128)).T


def around(at_ref, k, by, n):
    return lax.rem(at_ref[k] + (n + by), n)


def own_body(a_ref, o_ref):
    o_ref[0:32, :] = a_ref[...]


def join_body(b_ref, c_ref, d_ref, in_ref, o_ref):
    for k, ref in enumerate((b_ref, c_ref, d_ref)):
        o_ref[32 * k + 32 : 32 * k + 64, :] = ref[...]


def collect(at_ref, pieces, c_ref, ft_ref, fa_ref, fs_ref, cs_ref):
    for k, (by, parts) in enumerate(pieces):
        at = around(at_ref, 2, by, 8)
        for (ref, row), off in zip(parts, (0, -1, 1, 2)):
            place = pl.multiple_of(32 * around(at_ref, 3, off, 4), 32)
            ft_ref[at, pl.ds(place, 32), :] = ref[row : row + 32, :]
        piece = ft_ref[at]
        top = jnp.max(jnp.abs(piece), axis=0, keepdims=True).astype(F32)
        fa_ref[pl.ds(at, 1), :] = jnp.broadcast_to(jnp.max(top, axis=1, keepdims=True), (1, 128))
        fs_ref[:, 128 * k : 128 * k + 128] = piece.T
        cs_ref[:, 128 * k : 128 * k + 128] = c_ref[:, pl.ds(pl.multiple_of(at * 128, 128), 128)]


def product(f, c):
    return lax.dot_general(f, c, (((1,), (1,)), ((), ())), preferred_element_type=F32)


def whole(ref):
    return [(ref, 32 * k) for k in range(4)]


def accumulate(kin, k_ref, fs, cs):
    def block(b, carry):
        rows = pl.ds(pl.multiple_of(256 * b, 256), 256)
        s = product(fs[rows, :], cs[...])
        k_ref[rows, :] = s if kin is None else kin[rows, :] + s
        return carry

    lax.fori_loop(0, 4, block, 0)


def score0_body(at_ref, s_ref, c_ref, k_ref, ft_ref, fa_ref, fs, cs):
    collect(at_ref, [(0, whole(s_ref))], c_ref, ft_ref, fa_ref, fs, cs)
    accumulate(None, k_ref, fs, cs)


def score_body(by, at_ref, l, r, c_ref, kin, ftin, fain, k_ref, ft_ref, fa_ref, fs, cs):
    collect(at_ref, [(by, whole(l)), (-by, whole(r))], c_ref, ft_ref, fa_ref, fs, cs)
    accumulate(kin, k_ref, fs, cs)


def score4_body(at_ref, h0, h1, c_ref, kin, ftin, fain, k_ref, ft_ref, fa_ref, p_ref, fs, cs, tops, sums):
    far = (4, [(h0, 0), (h0, 32), (h1, 0), (h1, 32)])
    collect(at_ref, [far], c_ref, ft_ref, fa_ref, fs, cs)

    def scored(b):
        rows = pl.ds(pl.multiple_of(128 * b, 128), 128)
        s = kin[rows, :] + product(fs[rows, :], cs[...])
        k_ref[rows, :] = s
        tops[rows, :] = jnp.broadcast_to(jnp.max(s, axis=1, keepdims=True), (128, 128))

    def raised(b):
        rows = pl.ds(pl.multiple_of(128 * b, 128), 128)
        top, acc = tops[rows, :], jnp.zeros((128, 128), F32)
        for t in range(CB):
            cols = slice(128 * t, 128 * t + 128)
            e = jnp.exp(k_ref[rows, cols] - top)
            k_ref[rows, cols] = e
            acc = acc + e
        sums[rows, :] = acc

    def block(b, carry):
        raised(b)
        scored(b + 1)
        return carry

    scored(0)
    lax.fori_loop(0, RB - 1, block, 0)
    raised(RB - 1)
    lines = [tops[128 * b : 128 * b + 128, :].T[0:1] for b in range(RB)]
    lines += [jnp.sum(sums[128 * b : 128 * b + 128, :].T, axis=0, keepdims=True) for b in range(RB)]
    p_ref[...] = jnp.broadcast_to(jnp.concatenate(lines, axis=0)[None], p_ref.shape)


def columns(k_ref, scale, o_ref):
    acc = [jnp.zeros((8, 128), F32)] * CB
    for b in range(RB):
        rows = slice(128 * b, 128 * b + 128)
        by = down(scale[b : b + 1])
        for t in range(CB):
            part = k_ref[rows, 128 * t : 128 * t + 128] * by
            acc[t] = acc[t] + jnp.sum(part.reshape(16, 8, 128), axis=0)
    z = jnp.concatenate([jnp.sum(a, axis=0, keepdims=True) for a in acc], axis=0)
    o_ref[...] = jnp.broadcast_to(z[None], o_ref.shape)


def first_column_body(e_ref, mine_ref, a_ref, k_ref, o_ref, f_ref):
    peaks = e_ref[:, 0:RB, :]
    top = jnp.max(peaks, axis=0)
    total = jnp.sum(e_ref[:, RB : 2 * RB, :] * jnp.exp(peaks - top[None]), axis=0)
    fold = jnp.exp(mine_ref[0, 0:RB, :] - top)
    f_ref[...] = fold
    columns(k_ref, (a_ref[...] / total) * fold, o_ref)


def column_body(e_ref, f_ref, a_ref, k_ref, o_ref):
    scale = a_ref[...] / jnp.sum(e_ref[...], axis=0)
    columns(k_ref, scale * f_ref[...], o_ref)


def row_body(e_ref, f_ref, b_ref, k_ref, o_ref, *refs):
    scale = b_ref[...] / jnp.sum(e_ref[...], axis=0)
    acc_ref = refs[-1]
    if len(refs) > 1:
        refs[0][...] = scale
    small = scale * 2.0**-12

    def block(b, carry):
        rows = pl.ds(pl.multiple_of(128 * b, 128), 128)
        acc = jnp.zeros((128, 128), F32)
        for t in range(CB):
            acc = acc + k_ref[rows, 128 * t : 128 * t + 128] * small[t : t + 1]
        acc_ref[rows, :] = acc
        return carry

    lax.fori_loop(0, RB, block, 0)
    lines = [
        jnp.sum(acc_ref[128 * b : 128 * b + 128, :].T, axis=0, keepdims=True) for b in range(RB)
    ]
    y = jnp.concatenate(lines, axis=0) * (f_ref[...] * 2.0**12)
    o_ref[...] = jnp.broadcast_to(y[None], o_ref.shape)


def target(at_ref, by, side):
    return 2 * around(at_ref, 0, by, 4) + around(at_ref, 1, side, 2)


def product_of(at_ref, ft_ref, w_ref, o_ref, by, side):
    feats = ft_ref[target(at_ref, by, side)]
    o_ref[...] = jnp.dot(feats, w_ref[...], preferred_element_type=F32)


def weight_body(e_ref, f_ref, a_ref, c_ref, fa_ref, k_ref, w_ref, m_ref):
    scale = (a_ref[...] / jnp.sum(e_ref[...], axis=0)) * f_ref[...]
    acc = [jnp.zeros((8, 128), F32)] * CB
    for b in range(RB):
        rows = slice(128 * b, 128 * b + 128)
        by = down(scale[b : b + 1])
        for t in range(CB):
            cols = slice(128 * t, 128 * t + 128)
            part = (k_ref[rows, cols] * by) * c_ref[t : t + 1, :]
            acc[t] = acc[t] + jnp.sum(part.reshape(16, 8, 128), axis=0)
            w_ref[rows, cols] = part.astype(BF16)
    m_ref[0:CB, :] = jnp.concatenate([jnp.sum(a, axis=0, keepdims=True) for a in acc], axis=0)
    m_ref[CB : CB + 8, :] = fa_ref[...]


def limits(at_ref, m, by):
    return jnp.maximum(m[0:CB, :] * m[pl.ds(CB + target(at_ref, by, 0), 1), :], 2.0**-100)


def inverse(q):
    return 32768.0 / q


def chip_body(at_ref, ft_ref, w_ref, mine_ref, other_ref, o_ref, m_ref, i_ref):
    product_of(at_ref, ft_ref, w_ref, o_ref, 2, 0)
    m_ref[0:CB, :] = mine_ref[0:CB, :] + other_ref[0:CB, :]
    m_ref[CB : CB + 8, :] = jnp.maximum(mine_ref[CB : CB + 8, :], other_ref[CB : CB + 8, :])
    for k, by in enumerate((2, 1, 3)):
        i_ref[k] = inverse(limits(at_ref, m_ref, by))


def sides(at_ref, near, other):
    first = at_ref[1] == 0
    return jnp.where(first, near[...], other[...]), jnp.where(first, other[...], near[...])


def limits_of(at_ref, m, ref, by):
    ref[...] = m
    return limits(at_ref, ref, by)


def relay_body(at_ref, m0, near, other, i_ref, s_ref, tmp):
    for k, (m, by) in enumerate(zip(sides(at_ref, near, other), (1, 3))):
        q = limits_of(at_ref, m, tmp, by)
        s_ref[k] = q * (1.0 / 32768.0)
        i_ref[k] = inverse(q + limits(at_ref, m0, by))


def share_body(at_ref, m0, near, m2, other, t_ref, i_ref, s_ref, tmp):
    m1, m3 = sides(at_ref, near, other)
    total = (m0[0:CB, :] + m2[0:CB, :]) + (m1[0:CB, :] + m3[0:CB, :])
    t_ref[...] = total
    over = 1.0 / total
    i_ref[...] = over
    q1, q3 = (limits_of(at_ref, m, tmp, 0) * (1.0 / 32768.0) for m in (m1, m3))
    q2 = limits(at_ref, m2, 0) * (1.0 / 32768.0)
    for k, q in enumerate((q1, q3, q1 + q2, q3 + q2)):
        s_ref[k] = q * over


def product_body(which, at_ref, ft_ref, w_ref, *o_refs):
    for k, o_ref in enumerate(o_refs):
        product_of(at_ref, ft_ref, w_ref, o_ref, *which[k])


def assigned(features, centroids, row_weight, centroid_share):
    y, core, z, x = (lax.axis_index(n) for n in ("y", "core", "z", "x"))
    at = jnp.stack([y, core, z, x]).astype(jnp.int32)
    a = row_weight.reshape(RB, 128)
    share = centroid_share.reshape(CB, 128)

    own = after(features.T, at)

    def ring(x, by):
        return step(x, "z", by)

    def scores(body, outs, ins, depth, aliases=None, more=()):
        return call(
            body,
            outs,
            ins,
            scratch=[pltpu.VMEM((ROWS, depth), BF16), pltpu.VMEM((COLS, depth), BF16), *more],
            mib=16,
            aliases=aliases,
        )

    parts = []
    for by in (1, -1, 2):
        parts.append(step(own, "x", by))
    strip_shape = [((128, ROWS), BF16)]
    (strip,) = call(own_body, strip_shape, [own], mib=4)
    (strip,) = call(join_body, strip_shape, [*parts, strip], mib=4, aliases={3: 0})
    state = [((ROWS, COLS), F32), ((8, 128, ROWS), BF16), ((8, 128), F32)]
    right = [strip, ring(strip, 1)]
    left = [strip, ring(strip, -1)]
    kernel, ft, fa = scores(score0_body, state, [at, strip, centroids], 128)
    for k in (1, 2):
        right.append(ring(right[k], 1))
        left.append(ring(left[k], -1))
    far = [ring(right[3][:64], 1), ring(left[3][64:], -1)]
    for k in (1, 2, 3):
        kernel, ft, fa = scores(
            functools.partial(score_body, k),
            state,
            [at, left[k], right[k], centroids, kernel, ft, fa],
            256,
            {4: 0, 5: 1, 6: 2},
        )
    kernel, ft, fa, peaks = scores(
        score4_body,
        [*state, ((32, 2 * RB, 128), F32)],
        [at, *far, centroids, kernel, ft, fa],
        128,
        {4: 0, 5: 1, 6: 2},
        [pltpu.VMEM((ROWS, 128), F32)] * 2,
    )
    lines = [pltpu.VMEM((ROWS, 128), F32)]
    got = everyone(peaks, CENT)
    sums, fold = call(
        first_column_body, [((8, CB, 128), F32), ((RB, 128), F32)], [got, peaks, a, kernel], mib=8
    )
    for it in range(ITERS):
        rows, *cscale = call(
            row_body,
            [((32, RB, 128), F32)] + [((CB, 128), F32)] * (it == ITERS - 1),
            [everyone(sums, DP), fold, share, kernel],
            scratch=lines,
            mib=8,
        )
        got = everyone(rows, CENT)
        if it < ITERS - 1:
            (sums,) = call(column_body, [((8, CB, 128), F32)], [got, fold, a, kernel], mib=8)
    weights, mass = call(
        weight_body,
        [((ROWS, COLS), BF16), ((CB + 8, 128), F32)],
        [got, fold, a, *cscale, fa, kernel],
        mib=8,
    )

    other = step(mass, "core", 1)

    def products(which, where):
        return call(
            functools.partial(product_body, which),
            [((128, COLS), F32)] * len(which),
            [where, ft, weights],
            mib=16,
        )

    def send(x, by):
        return step(x.astype(jnp.float16), "y", by)

    low, high = slice(0, 64), slice(64, 128)
    (give,) = products([(2, 1)], at)
    theirs = step(give, "core", 1)
    mine, chip, packs = call(
        chip_body,
        [((128, COLS), F32), ((CB + 8, 128), F32), ((3, CB, 128), F32)],
        [after(at, give), ft, weights, mass, other],
        mib=16,
    )
    packs = packs.reshape(3, 1, COLS)
    near = step_apart(chip)
    other_near = step(near, "core", 1)
    far_mass = step_apart(near)
    up = ((mine[low] + theirs[low]) * packs[0]).astype(jnp.float16)
    down_ = ((mine[high] + theirs[high]) * packs[0]).astype(jnp.float16)
    first = (send(up, 1), send(down_, 3))
    gives = products([(1, 1), (3, 1)], after(at, up, down_))
    theirs = [step(g, "core", 1) for g in gives]
    mines = products([(1, 0), (3, 0)], after(at, *gives))
    up = ((mines[0][high] + theirs[0][high]) * packs[1]).astype(jnp.float16)
    down_ = ((mines[1][low] + theirs[1][low]) * packs[2]).astype(jnp.float16)
    second = (send(up, 1), send(down_, 3))
    repacks, unpacks = call(
        relay_body,
        [((2, CB, 128), F32)] * 2,
        [at, chip, near, other_near],
        scratch=[pltpu.VMEM((CB + 8, 128), F32)],
        mib=4,
    )
    repacks, unpacks = repacks.reshape(2, 1, COLS), unpacks.reshape(2, 1, COLS)
    give, mine0 = products([(0, 1), (0, 0)], at)
    theirs0 = step(give, "core", 1)
    total, over, shares = call(
        share_body,
        [((CB, 128), F32), ((CB, 128), F32), ((4, CB, 128), F32)],
        [at, chip, near, far_mass, other_near],
        scratch=[pltpu.VMEM((CB + 8, 128), F32)],
        mib=4,
    )
    mines, theirs, *_ = lax.optimization_barrier((mines, theirs, up, down_))
    up = mines[0][low] + theirs[0][low] + first[0].astype(F32) * unpacks[0]
    down_ = mines[1][high] + theirs[1][high] + first[1].astype(F32) * unpacks[1]
    third = (send(up * repacks[0], 1), send(down_ * repacks[1], 3))

    over, shares = over.reshape(1, COLS), shares.reshape(4, 1, COLS)
    own_part = (mine0 + theirs0) * over
    sent = [second[1].astype(F32) * shares[1], second[0].astype(F32) * shares[0]]
    base = lax.optimization_barrier(own_part + jnp.concatenate(sent, axis=0))
    last = [third[0].astype(F32) * shares[2], third[1].astype(F32) * shares[3]]
    return base + jnp.concatenate(last, axis=0), total.reshape(COLS)


def solution(mesh):
    split = Mesh(mesh.devices.reshape(4, 2, 8, 4), ("y", "core", "z", "x"))
    return jax.shard_map(
        assigned,
        mesh=split,
        in_specs=(P(DP, CENT), P(CENT, None), P(DP), P(CENT)),
        out_specs=(P(DP, CENT), P(CENT)),
        check_vma=False,
    )
```
